32 devices in a mesh: dom: 8 (over y, x, core), head: 4 (over z).
Axes of the slice: x: 2, y: 2, z: 4, core: 2. Of those that a mesh axis runs over, the one named last changes fastest.
Arguments:
- features: bfloat16 [25, 128, 4096], P(None, None, ('dom', 'head')), may hold values from -14 to 14
- positions: float32 [3, 4096], P(None, 'dom'), may hold values from 0 to 3
- penalty: float32 [16], replicated, may hold values from 0.01 to 0.5
- qk_weight: bfloat16 [128, 2048], replicated, may hold values from -0.5 to 0.5
- value_weight: bfloat16 [5, 128, 128], replicated, may hold values from -0.5 to 0.5
- output_weight: bfloat16 [5, 128, 128], replicated, may hold values from -0.5 to 0.5
- frames: float32 [64, 25, 25], replicated, may hold values from -3 to 3, as said below
- frame_index: int32 [64], P('dom'), may hold values from 0 to 63
- neighbours: int32 [64, 8], P('dom'), may hold values from 0 to 63, as said below
- counts: int32 [64], P('dom'), may hold values from 1 to 8
- cotangent: bfloat16 [25, 128, 4096], P(None, None, ('dom', 'head')), may hold values from -6 to 6
Outputs:
- updated: bfloat16 [25, 128, 4096], P(None, None, ('dom', 'head'))
- forces: float32 [3, 4096], P(None, ('dom', 'head'))
The draws below stay inside these ranges and needn't reach their ends.
Inputs may be any that keep to these rules, and one draw needn't show every extreme that they name: `frames`: entries outside the diagonal blocks of components of one degree are zero. `neighbours`: row b holds 8 distinct blocks (b + o) mod 64 with |o| <= 4; the slots at and beyond counts[b] are padding.
All inputs are finite; a program needn't handle non-finite values.
Results may differ from the reference program's by a relative error of at most 0.0037.
The reference program's roundings to bfloat16 on the way count: a program that leaves them out, or rounds other values in their place, can miss the bound.
Values may be sent and summed in bfloat16 or wider, within the bound.
A program may use at most 64 MiB of HBM per device.

```python
import math
import jax
import jax.numpy as jnp
from jax import lax

COMP = 25
LDEG = 5
CH = 128
HEADS = 16
ALPHA = 64
BLOCK = 64
NBR = 8
REACH = 4
NFRAME = 64
ATOMS = 4096
BLOCKS = 64


def draw_features(key, part):
    folded = jax.random.fold_in(key, 101)
    first_key = jax.random.fold_in(folded, 0)
    return jnp.clip(jax.random.normal(first_key, (COMP, CH, ATOMS), jnp.float32), -6.0, 6.0).astype(jnp.bfloat16)


def draw_frames(key, part):
    folded = jax.random.fold_in(key, 202)
    index_comp = jnp.arange(COMP)
    degrees = jnp.sum((index_comp[:, None] >= (jnp.arange(1, LDEG) ** 2)[None, :]).astype(jnp.int32), axis=1)
    same_degree = (degrees[:, None] == degrees[None, :]).astype(jnp.float32)
    widths = jnp.sqrt(2.0 * degrees.astype(jnp.float32) + 1.0)[None, :, None]
    noise_draw = jnp.clip(jax.random.normal(folded, (NFRAME, COMP, COMP), jnp.float32), -4.0, 4.0)
    return (jnp.eye(COMP, dtype=jnp.float32)[None] + 0.5 * noise_draw / widths) * same_degree[None]


def draw_neighbours(key, part):
    folded = jax.random.fold_in(key, 303)
    spanned = 2 * REACH + 1
    raw_scores = jax.random.randint(folded, (BLOCKS, spanned), 0, 1 << 20) * spanned + jnp.arange(spanned)[None, :]
    ordering = jnp.argsort(raw_scores, axis=1)
    offsets = ordering[:, :NBR] - REACH
    return jnp.mod(jnp.arange(BLOCKS)[:, None] + offsets, BLOCKS).astype(jnp.int32)


def draw_counts(key, part):
    folded = jax.random.fold_in(key, 404)
    first_key, second_key, third_key = jax.random.split(folded, 3)
    values_drawn = jax.random.randint(first_key, (BLOCKS,), 1, NBR + 1)
    fullest = jax.random.randint(second_key, (), 0, BLOCKS)
    emptiest = jnp.mod(fullest + 1 + jax.random.randint(third_key, (), 0, BLOCKS - 1), BLOCKS)
    return values_drawn.at[fullest].set(NBR).at[emptiest].set(1).astype(jnp.int32)


def plant(result, own_key, smallest, largest):
    index_at = [jax.random.randint(jax.random.fold_in(own_key, axis), (), 0, length) for axis, length in enumerate(result.shape)]
    main_axis = result.shape.index(max(result.shape))
    beside = index_at[:main_axis] + [(index_at[main_axis] + 1) % result.shape[main_axis]] + index_at[main_axis + 1:]
    return result.at[tuple(index_at)].set(smallest).at[tuple(beside)].set(largest)


def shard_levels(key, extent, cuts, least, high):
    def one(axis_at, shards_of):
        heights = jax.random.uniform(jax.random.fold_in(jax.random.fold_in(key, 6), axis_at), (shards_of,), jnp.float32, least / len(cuts), high / len(cuts))
        return jnp.repeat(jnp.exp(heights), extent[axis_at] // shards_of).reshape((-1,) + (1,) * (len(extent) - axis_at - 1))

    loudness = one(*cuts[0])
    for cut in cuts[1:]:
        loudness = loudness * one(*cut)
    return loudness


def gaussian(rng, dims, deviation, most, cuts=(), kind=jnp.bfloat16):
    result = jax.random.normal(rng, dims, jnp.float32) * deviation
    if len(cuts) > 0:
        result = shard_levels(rng, dims, cuts, -0.22, 0.18) * result
    return jnp.clip(result, min=-most, max=most).astype(kind)


def setup_inputs(seed: int = 0) -> dict:
    streams_of = jax.random.split(jax.random.key(seed), 12)
    return {
        "features": draw_features(jax.random.fold_in(streams_of[11], 71), 0),
        "positions": jnp.clip(3.0 * jax.random.uniform(streams_of[1], (3, ATOMS), jnp.float32) ** shard_levels(streams_of[1], (3, ATOMS), ((1, 8),), -0.2, 0.2), 0.0, 3.0),
        "penalty": jnp.clip(jnp.exp(jax.random.uniform(streams_of[2], (HEADS,), jnp.float32, math.log(0.01), math.log(0.5))), 0.01, 0.5),
        "qk_weight": gaussian(streams_of[3], (CH, 2 * HEADS * ALPHA), CH ** -0.5, 0.5),
        "value_weight": gaussian(streams_of[4], (LDEG, CH, CH), CH ** -0.5, 0.5),
        "output_weight": gaussian(streams_of[5], (LDEG, CH, CH), CH ** -0.5, 0.5),
        "frames": draw_frames(jax.random.fold_in(streams_of[11], 71), 0),
        "frame_index": plant(jax.random.randint(streams_of[7], (BLOCKS,), 0, NFRAME), jax.random.fold_in(streams_of[7], 1), 0, NFRAME - 1).astype(jnp.int32),
        "neighbours": draw_neighbours(jax.random.fold_in(streams_of[11], 71), 0),
        "counts": draw_counts(jax.random.fold_in(streams_of[11], 71), 0),
        "cotangent": gaussian(streams_of[10], (COMP, CH, ATOMS), 1.0, 6.0, ((2, 32),)),
    }


NEG_FILL = -1e+30

def degree_table():
    components = jnp.arange(COMP)
    degrees = lax.optimization_barrier(jnp.sum((components[:, None] >= (jnp.arange(1, LDEG) ** 2)[None, :]).astype(jnp.int32), axis=1))
    orders = components - degrees * degrees - degrees
    return (jnp.abs(orders) <= 2).astype(jnp.float32)

def projectors(frames):
    kept_mask = degree_table()
    return jnp.einsum('fji,j,fjk->fik', frames, kept_mask, frames, precision=lax.Precision.HIGHEST)

def mix_degrees(operand, weights, reverse):
    pieces = []
    for degree in range(weights.shape[0]):
        sliced = operand[degree * degree:(degree + 1) * (degree + 1)].astype(jnp.float32)
        matrix = weights[degree].astype(jnp.float32)
        if reverse:
            pieces.append(jnp.einsum('koa,co->kca', sliced, matrix))
        else:
            pieces.append(jnp.einsum('kca,co->koa', sliced, matrix))
    return jnp.concatenate(pieces, 0)

def pick_group(nblocks, heads_here):
    chosen = 1
    for candidate in range(1, nblocks + 1):
        if nblocks % candidate == 0 and candidate * BLOCK * heads_here <= 512:
            chosen = candidate
    return chosen

def reference(features, positions, penalty, qk_weight, value_weight, output_weight, frames, frame_index, neighbours, counts, cotangent):
    atoms_all = features.shape[2]
    blocks_all = atoms_all // BLOCK
    head_width = CH // HEADS
    query_rows = HEADS * ALPHA
    projections = projectors(frames)
    queries_keys = jnp.dot(qk_weight.T, features[0], preferred_element_type=jnp.float32).astype(jnp.bfloat16)
    values = mix_degrees(features, value_weight, False).astype(jnp.bfloat16)
    grads = mix_degrees(cotangent, output_weight, True).astype(jnp.bfloat16)
    query_blocks = queries_keys[:query_rows].reshape(HEADS, ALPHA, blocks_all, BLOCK)
    key_blocks = queries_keys[query_rows:].reshape(HEADS, ALPHA, blocks_all, BLOCK)
    value_blocks = values.reshape(COMP, HEADS, head_width, blocks_all, BLOCK)
    grad_blocks = grads.reshape(COMP, HEADS, head_width, blocks_all, BLOCK)
    point_blocks = positions.reshape(3, blocks_all, BLOCK)
    usable = jnp.arange(NBR)[None, :] < counts[:, None]
    matrices = projections[frame_index]
    group_size = pick_group(blocks_all, 1)
    inverse_root = 1.0 / math.sqrt(ALPHA)

    def group_step(state_now, begin_at):
        attended_all, query_forces, ghost_forces = state_now
        slot_blocks = lax.dynamic_slice_in_dim(neighbours, begin_at, group_size, 0)
        query_group = lax.dynamic_slice_in_dim(query_blocks, begin_at, group_size, 2).astype(jnp.float32)
        key_group = jnp.take(key_blocks, slot_blocks, axis=2).astype(jnp.float32)
        value_group = jnp.take(value_blocks, slot_blocks, axis=3).astype(jnp.float32)
        grad_group = lax.dynamic_slice_in_dim(grad_blocks, begin_at, group_size, 3).astype(jnp.float32)
        query_points = lax.dynamic_slice_in_dim(point_blocks, begin_at, group_size, 1)
        key_points = jnp.take(point_blocks, slot_blocks, axis=1)
        live_slots = lax.dynamic_slice_in_dim(usable, begin_at, group_size, 0)
        group_mats = lax.dynamic_slice_in_dim(matrices, begin_at, group_size, 0)
        scores = jnp.einsum('hagi,hagsj->hgisj', query_group, key_group) * inverse_root
        separation = query_points[:, :, :, None, None] - key_points[:, :, None, :, :]
        distance = lax.optimization_barrier(jnp.sum(separation * separation, axis=0))
        logits = scores - penalty[:, None, None, None, None] * distance[None]
        slot_mask = live_slots[None, :, None, :, None]
        logits = jnp.where(slot_mask, logits, NEG_FILL)
        peaks = lax.optimization_barrier(jnp.max(logits, axis=(3, 4), keepdims=True))
        exponent = jnp.where(slot_mask, jnp.exp(logits - peaks), 0.0)
        attention = exponent / lax.optimization_barrier(jnp.sum(exponent, axis=(3, 4), keepdims=True))
        rounded = lax.optimization_barrier(attention.astype(jnp.bfloat16)).astype(jnp.float32)
        aggregate = jnp.einsum('hgisj,khdgsj->khdgi', rounded, value_group)
        attended = jnp.einsum('gkl,lhdgi->khdgi', group_mats, aggregate, precision=lax.Precision.HIGHEST).astype(jnp.bfloat16)
        rotated = jnp.einsum('glk,lhdgi->khdgi', group_mats, grad_group, precision=lax.Precision.HIGHEST)
        rotated = lax.optimization_barrier(rotated.astype(jnp.bfloat16)).astype(jnp.float32)
        weight_grads = jnp.einsum('khdgi,khdgsj->hgisj', rotated, value_group)
        logit_grads = attention * (weight_grads - lax.optimization_barrier(jnp.sum(attention * weight_grads, axis=(3, 4), keepdims=True)))
        total = lax.optimization_barrier(jnp.sum(2.0 * penalty[:, None, None, None, None] * logit_grads, axis=0))
        force_query = lax.optimization_barrier(jnp.sum(total[None] * separation, axis=(3, 4)))
        force_key = -lax.optimization_barrier(jnp.sum(total[None] * separation, axis=2))
        attended_all = lax.dynamic_update_slice_in_dim(attended_all, attended, begin_at, 3)
        query_forces = lax.dynamic_update_slice_in_dim(query_forces, force_query, begin_at, 1)
        ghost_forces = ghost_forces.at[:, slot_blocks.reshape(-1)].add(force_key.reshape(3, -1, BLOCK))
        return ((attended_all, query_forces, ghost_forces), None)
    initial = (jnp.zeros((COMP, HEADS, head_width, blocks_all, BLOCK), jnp.bfloat16), jnp.zeros((3, blocks_all, BLOCK), jnp.float32), jnp.zeros((3, blocks_all, BLOCK), jnp.float32))
    begins = jnp.arange(0, blocks_all, group_size).astype(jnp.int32)
    final_state, unused_out = lax.scan(group_step, initial, begins)
    attended_all, query_forces, ghost_forces = final_state
    attended_atoms = attended_all.reshape(COMP, CH, atoms_all)
    updated = (features.astype(jnp.float32) + mix_degrees(attended_atoms, output_weight, False)).astype(jnp.bfloat16)
    forces = (query_forces + ghost_forces).reshape(3, atoms_all)
    return (updated, forces)
```

```python
import functools
import math

import jax
import jax.numpy as jnp
from jax import lax
from jax.experimental import pallas as pl
from jax.experimental.pallas import tpu as pltpu
from jax.sharding import PartitionSpec as P

BLOCK = 64
REACH = 4
FAR = 1e30
VMEM_LIMIT = 63 * 1024 * 1024


def degree_of(k):
    return math.isqrt(k)


def pair_table(comp):
    pairs = []
    for k in range(comp):
        l = degree_of(k)
        for m in range(l * l, (l + 1) * (l + 1)):
            pairs.append((k, m))
    return pairs


def vmem():
    return pl.BlockSpec(memory_space=pltpu.VMEM)


def dot(a, b, ca, cb):
    return lax.dot_general(
        a, b, (((ca,), (cb,)), ((), ())), preferred_element_type=jnp.float32
    )


def rotated_rows(coef, tile, comp, source, k, turned):
    index_of = {pair: n for n, pair in enumerate(pair_table(comp))}
    l = degree_of(k)
    total = None
    for m in range(l * l, (l + 1) * (l + 1)):
        row = index_of[(m, k) if turned else (k, m)]
        term = coef[tile, row : row + 1, :] * source(m)
        total = term if total is None else total + term
    return total


def paired(low, high, head_width):
    rows, atoms = low.shape
    shape = (rows // head_width, head_width, atoms)
    return jnp.concatenate([low.reshape(shape), high.reshape(shape)], axis=1).astype(jnp.bfloat16)


def fused_kernel(
    heads,
    alpha,
    doms,
    ranks,
    group,
    penalty,
    frame_index,
    neighbours,
    counts,
    features_in,
    cotangent_in,
    value_weight_in,
    output_weight_in,
    qk_weight_in,
    frames_in,
    positions_in,
    updated,
    force,
    packed,
    vals,
    scal,
    back,
    turned_out,
    turned_in,
    finished,
    arrived,
    own_points,
    points,
    points_t,
    coef,
    mask,
    distance_s,
    keys_s,
    queries_s,
    aggregate_s,
    attention_s,
    rounded_s,
    total_s,
    forces,
    force_in,
    scal_sems,
    scal_forward_sems,
    value_sems,
    forward_sems,
    back_sems,
    finished_sems,
    force_sems,
    point_sems,
    features,
    cotangent,
    value_weight,
    output_weight,
    q_weight,
    k_weight,
    frames,
    positions,
    load_sems,
):
    comp, channels, atoms = features.shape
    head_width = channels // (group * heads)
    half = channels // group
    slots = 3 * group
    window = 2 * group + 1
    per_tile = atoms // BLOCK
    groups = ranks // group
    relay = groups == 2
    sent = (comp - 1) * head_width
    head_columns = heads * alpha
    me = lax.axis_index("head")
    dom = lax.axis_index("dom")
    mine = lax.rem(me, group)
    place = lax.div(me, group)
    up = lax.rem(dom + 1, doms)
    down = lax.rem(dom + doms - 1, doms)

    loads = [
        pltpu.make_async_copy(src, dst, load_sems.at[n])
        for n, (src, dst) in enumerate(
            [
                (features_in, features),
                (value_weight_in, value_weight),
                (positions_in, positions),
                (frames_in, frames),
                (cotangent_in, cotangent),
                (output_weight_in, output_weight),
                (
                    qk_weight_in.at[:, pl.ds(pl.multiple_of(mine * head_columns, 128), head_columns)],
                    q_weight,
                ),
                (
                    qk_weight_in.at[
                        :,
                        pl.ds(
                            pl.multiple_of((group + mine) * head_columns, 128), head_columns
                        ),
                    ],
                    k_weight,
                ),
            ]
        )
    ]
    for load in loads:
        load.start()

    def member(shift):
        return lax.rem(mine + shift, group)

    def group_at(shift):
        at = lax.rem(dom * groups + place + doms * groups + shift, doms * groups)
        return lax.div(at, groups), lax.rem(at, groups)

    others = []
    for shift, base in ((1, 2 * group), (-1, 0)):
        at_dom, at_place = group_at(shift)
        for j in range(group):
            n = member(j)
            others.append(
                (
                    (at_dom, at_place * group + n),
                    n,
                    base + n,
                    2 * group - base + mine,
                    2 * group - base + n,
                )
            )
    partners = []
    for j in range(1, group):
        n = member(j)
        partners.append(((dom, place * group + n), n, group + n, group + mine, group + n))
    others = others + partners

    far = 2 * group * (1 - place)
    near = 2 * group * place
    if relay:
        beside = lax.rem(dom + doms + 1 - 2 * place, doms)
        links = []
        for j in range(group):
            n = member(j)
            links.append(((dom, (1 - place) * group + n), n, far + n, near + mine, far + n))
        links = links + partners
    else:
        links = others

    def remote(src, dst, sems, at, device):
        return pltpu.make_async_remote_copy(
            src_ref=src,
            dst_ref=dst,
            send_sem=sems.at[(0,) + at],
            recv_sem=sems.at[(1,) + at],
            device_id=device,
            device_id_type=pl.DeviceIdType.MESH,
        )

    barrier = pltpu.get_barrier_semaphore()
    greeted = [other[0] for other in others] + [(up, me), (down, me)]
    for device in greeted:
        pl.semaphore_signal(
            barrier, inc=1, device_id=device, device_id_type=pl.DeviceIdType.MESH
        )

    def scal_copy(n):
        device, _, _, there, _ = links[n]
        return remote(scal.at[group + mine], scal.at[there], scal_sems, (n,), device)

    def scal_arrival(n):
        device, _, _, _, here = links[n]
        return remote(scal.at[group + mine], scal.at[here], scal_sems, (n,), device)

    def scal_forward(j):
        n = member(j)
        return remote(
            scal.at[far + n], scal.at[near + n], scal_forward_sems, (j,), (beside, me)
        )

    def value_copy(n, h):
        device, member_there, _, there, _ = links[n]
        return remote(
            packed.at[member_there * heads + h],
            vals.at[there, h, pl.ds(0, sent)],
            value_sems,
            (n, h),
            device,
        )

    def value_arrival(n, h):
        device, member_there, _, _, here = links[n]
        return remote(
            packed.at[member_there * heads + h],
            vals.at[here, h, pl.ds(0, sent)],
            value_sems,
            (n, h),
            device,
        )

    def value_forward(j, h):
        n = member(j)
        return remote(
            vals.at[far + n, h, pl.ds(0, sent)],
            vals.at[near + n, h, pl.ds(0, sent)],
            forward_sems,
            (j, h),
            (beside, me),
        )

    def back_copy(n, h):
        device, member_there, _, _, _ = partners[n]
        return remote(
            turned_out.at[member_there * heads + h], turned_in.at[mine, h], back_sems, (n, h), device
        )

    def back_arrival(n, h):
        device, member_there, _, _, _ = partners[n]
        return remote(
            turned_out.at[member_there * heads + h],
            turned_in.at[member_there, h],
            back_sems,
            (n, h),
            device,
        )

    def finished_rows(of, c):
        return pl.ds(pl.multiple_of(of * half + c * 2 * head_width, 16), 2 * head_width)

    def finished_copy(n, c):
        device, member_there, _, _, _ = partners[n]
        return remote(
            finished.at[n, c], arrived.at[:, finished_rows(mine, c)], finished_sems, (n, c), device
        )

    def finished_arrival(n, c):
        device, member_there, _, _, _ = partners[n]
        return remote(
            finished.at[n, c],
            arrived.at[:, finished_rows(member_there, c)],
            finished_sems,
            (n, c),
            device,
        )

    def force_copy(n):
        device, _, here, _, _ = others[n]
        return remote(forces.at[here], force_in.at[n], force_sems, (n,), device)

    if relay:
        point_copies = [
            (
                None,
                remote(
                    own_points.at[pl.ds((ranks - group) * (1 - place), group)],
                    points.at[pl.ds(near, group)],
                    point_sems,
                    (0,),
                    (beside, me),
                ),
            )
        ]
    else:
        point_copies = [
            (
                place == 0,
                remote(
                    own_points.at[pl.ds(ranks - group, group)],
                    points.at[pl.ds(0, group)],
                    point_sems,
                    (0,),
                    (up, me),
                ),
            ),
            (
                place == groups - 1,
                remote(
                    own_points.at[pl.ds(0, group)],
                    points.at[pl.ds(2 * group, group)],
                    point_sems,
                    (1,),
                    (down, me),
                ),
            ),
        ]

    def for_points(act):
        for holds, copy in point_copies:
            if holds is None:
                act(copy)
            else:
                pl.when(holds)(functools.partial(act, copy))

    for load in loads[:3]:
        load.wait()
    scal[group + mine] = features[0]
    own_points[...] = jnp.zeros_like(own_points)
    for t in range(ranks):
        own_points[t, : positions.shape[0]] = positions[:, t * atoms : (t + 1) * atoms]
    for j in range((comp - 1) // 2):
        low, high = 2 * j + 1, 2 * j + 2
        packed[:, 2 * j * head_width : 2 * (j + 1) * head_width, :] = paired(
            dot(value_weight[degree_of(low)], features[low], 0, 0),
            dot(value_weight[degree_of(high)], features[high], 0, 0),
            head_width,
        )

    pl.semaphore_wait(barrier, len(greeted))

    for n in range(len(links)):
        scal_copy(n).start()
    for_points(lambda copy: copy.start())
    lead = 2
    for h in range(lead):
        for n in range(len(links)):
            value_copy(n, h).start()

    vals[group + mine, :, :sent] = packed[pl.ds(mine * heads, heads)]
    if relay:
        points[pl.ds(group * (1 - place), ranks)] = own_points[...]
    else:
        for s in range(slots):
            t = group * place - group + s

            @pl.when(jnp.logical_and(t >= 0, t < ranks))
            def _():
                points[s] = own_points[t]

    loads[3].wait()
    total_blocks = doms * ranks * per_tile
    lane = lax.broadcasted_iota(jnp.int32, (frames.shape[2], atoms), 1)
    frame_row = lax.broadcasted_iota(jnp.int32, (frames.shape[2], atoms), 0)
    slot_of = lax.broadcasted_iota(jnp.int32, (1, window * atoms), 1) // BLOCK

    def tables(q, carry):
        t = place * group + q
        points_t[q] = own_points[t].T
        wanted = jnp.zeros_like(lane) + frame_index[t * per_tile]
        for r in range(1, per_tile):
            wanted = jnp.where(lane < r * BLOCK, wanted, frame_index[t * per_tile + r])
        onehot = (frame_row == wanted).astype(jnp.float32)
        at = 0
        for l in range(degree_of(comp - 1) + 1):
            first, last = l * l, (l + 1) * (l + 1)
            kept = [
                lax.dot_general(
                    frames[j],
                    onehot,
                    (((1,), (0,)), ((), ())),
                    precision=lax.Precision.HIGHEST,
                    preferred_element_type=jnp.float32,
                )
                for j in range(first, last)
                if abs(j - first - l) <= 2
            ]
            for k in range(first, last):
                rows = None
                for matrix in kept:
                    term = matrix[k : k + 1, :] * matrix[first:last, :]
                    rows = term if rows is None else rows + term
                coef[q, at : at + last - first, :] = rows
                at += last - first
        for r in range(per_tile):
            block = t * per_tile + r
            hidden = jnp.full((1, window * atoms), FAR, jnp.float32)
            shift = r + group * per_tile - REACH
            for s in range(neighbours.shape[1]):
                offset = lax.rem(
                    neighbours[block, s]
                    - (dom * ranks * per_tile + block)
                    + REACH
                    + total_blocks,
                    total_blocks,
                )
                spot = jnp.where(counts[block] > s, offset + shift, -1)
                hidden = jnp.where(slot_of == spot, 0.0, hidden)
            mask[q, r : r + 1, :] = hidden
        return carry

    lax.fori_loop(0, group, tables, 0)

    for load in loads[4:]:
        load.wait()
    for k in range(comp):
        back[k] = (
            dot(output_weight[degree_of(k)], cotangent[k], 1, 0)
            .astype(jnp.bfloat16)
            .astype(jnp.float32)
        )
    strip = 4 * head_width

    def turn(i, carry):
        rows = pl.ds(pl.multiple_of(i * strip, strip), strip)

        def rotated(k):
            return rotated_rows(coef, mine, comp, lambda m: back[m, rows, :], k, True)

        into = pl.ds(i * 4, 4)
        for j in range((comp - 1) // 2):
            turned_out[into, 2 * j * head_width : 2 * (j + 1) * head_width, :] = paired(
                rotated(2 * j + 1), rotated(2 * j + 2), head_width
            )
        first = rotated(0)
        turned_out[into, sent : sent + 2 * head_width, :] = paired(
            first, jnp.zeros_like(first), head_width
        )
        return carry

    lax.fori_loop(0, channels // strip, turn, 0)

    for h in range(lead):
        for n in range(len(partners)):
            back_copy(n, h).start()
    for h in range(lead, heads):
        for n in range(len(links)):
            value_copy(n, h).start()
        for n in range(len(partners)):
            back_copy(n, h).start()
    turned_in[mine] = turned_out[pl.ds(mine * heads, heads)]

    for n in range(len(links)):
        scal_arrival(n).wait_recv()
    if relay:
        for j in range(group):
            scal_forward(j).start()

    def prepare(slot, carry):
        tile = scal[slot]
        mixed = dot(value_weight[0], tile, 0, 0)
        chosen = mixed[:half]
        for n in range(1, group):
            chosen = jnp.where(mine == n, mixed[n * half : (n + 1) * half], chosen)
        vals[slot, :, sent : sent + 2 * head_width, :] = paired(
            chosen, jnp.zeros_like(chosen), head_width
        )
        keys = dot(k_weight[...], tile, 0, 0)
        keys_s[slot] = keys.reshape(heads, alpha, atoms).astype(jnp.bfloat16)
        return carry

    scale = 1.0 / math.sqrt(alpha)

    def ask(q, carry):
        turned = scal[group + q].astype(jnp.float32).T.astype(jnp.bfloat16)
        for h in range(heads):
            asked = dot(turned, q_weight[:, h * alpha : (h + 1) * alpha], 1, 0)
            queries_s[q, h] = (asked.astype(jnp.bfloat16).astype(jnp.float32) * scale).astype(
                jnp.bfloat16
            )
        return carry

    lax.fori_loop(0, group, ask, 0)
    if relay:
        start = group * (1 - place)
        lax.fori_loop(start, start + 2 * group, prepare, 0)
        for j in range(group):
            scal_forward(j).wait_recv()
        lax.fori_loop(near, near + group, prepare, 0)
    else:
        lax.fori_loop(0, slots, prepare, 0)
    for_points(lambda copy: copy.wait_recv())

    def windowed(q, get):
        return jnp.concatenate([get(q + w) for w in range(window)], axis=-1)

    def attend(q, carry):
        distance = None
        for c in range(3):
            row = windowed(q, lambda s: points[s, c : c + 1, :])
            apart = points_t[q, :, c : c + 1] - row
            distance = apart * apart if distance is None else distance + apart * apart
        hidden = jnp.concatenate(
            [
                jnp.broadcast_to(mask[q, r : r + 1, :], (BLOCK, window * atoms))
                for r in range(per_tile)
            ],
            axis=0,
        )
        distance_s[...] = jnp.maximum(distance, hidden)
        total_s[q] = jnp.zeros_like(distance)

        def head(c, carry):
            for h in (2 * c, 2 * c + 1):
                keys = windowed(q, lambda s: keys_s[s, h])
                strength = penalty[mine * heads + h]
                logits = dot(queries_s[q, h], keys, 1, 0) - strength * distance_s[...]
                peaks = jnp.max(logits, axis=1, keepdims=True)
                exponent = jnp.exp(logits - peaks)
                inverse = 1.0 / jnp.sum(exponent, axis=1, keepdims=True)
                attention = exponent * inverse
                attention_s[q, h] = attention
                rounded_s[q, h] = attention.astype(jnp.bfloat16)
            return carry

        return lax.fori_loop(0, heads // 2, head, carry)

    lax.fori_loop(0, group, attend, 0)

    crossing = len(links) - len(partners)

    def receive(h):
        for n in range(crossing):
            value_arrival(n, h).wait_recv()
        if relay:
            for j in range(group):
                value_forward(j, h).start()

    receive(0)

    def pair(c, carry):
        for part in range(2):
            h = 2 * c + part

            @pl.when(h + 1 < heads)
            def _():
                receive(h + 1)

            if relay:
                for j in range(group):
                    value_forward(j, h).wait_recv()
            for n in range(len(partners)):
                value_arrival(crossing + n, h).wait_recv()
                back_arrival(n, h).wait_recv()

            strength = 2.0 * penalty[mine * heads + h]

            def tile(q, carry):
                values = windowed(q, lambda s: vals[s, h])
                aggregate_s[q, part] = dot(values, rounded_s[q, h], 1, 1)
                turned = turned_in[q, h].astype(jnp.float32).T.astype(jnp.bfloat16)
                weight_grads = dot(turned, values, 1, 0)
                attention = attention_s[q, h]
                weighted = attention * weight_grads
                mean = jnp.sum(weighted, axis=1, keepdims=True)
                total_s[q] = total_s[q] + strength * (weighted - attention * mean)
                return carry

            lax.fori_loop(0, group, tile, 0)

        def rows_of(k):
            return (k - 1) * head_width if k else sent

        def rotated(q, k):
            def source(m):
                at = rows_of(m)
                return jnp.concatenate(
                    [aggregate_s[q, part, at : at + head_width, :] for part in range(2)], axis=0
                )

            return rotated_rows(coef, q, comp, source, k, False).astype(jnp.bfloat16)

        for n in range(len(partners)):
            q = partners[n][1]
            for k in range(comp):
                finished[n, c, k] = rotated(q, k)
            finished_copy(n, c).start()
        for k in range(comp):
            arrived[k, finished_rows(mine, c), :] = rotated(mine, k)
        return carry

    lax.fori_loop(0, heads // 2, pair, 0)

    forces[...] = jnp.zeros_like(forces)
    lane_square = lax.broadcasted_iota(jnp.int32, (atoms, atoms), 1)

    def pull(q, carry):
        total = total_s[q]
        own = jnp.zeros((atoms, atoms), jnp.float32)
        theirs = []
        for c in range(3):
            row = windowed(q, lambda s: points[s, c : c + 1, :])
            weighted = total * (points_t[q, :, c : c + 1] - row)
            own = jnp.where(lane_square == c, jnp.sum(weighted, axis=1, keepdims=True), own)
            theirs.append(jnp.sum(weighted, axis=0, keepdims=True))
        own = own.T
        for c in range(3):
            forces[q + group, c : c + 1, :] = forces[q + group, c : c + 1, :] + own[c : c + 1]
            for w in range(window):
                forces[q + w, c : c + 1, :] = (
                    forces[q + w, c : c + 1, :] - theirs[c][:, w * atoms : (w + 1) * atoms]
                )
        return carry

    lax.fori_loop(0, group, pull, 0)
    for n in range(len(others)):
        force_copy(n).start()

    for n in range(len(partners)):
        for c in range(heads // 2):
            finished_arrival(n, c).wait_recv()
    for k in range(comp):
        mixed = dot(output_weight[degree_of(k)], arrived[k], 0, 0)
        updated[k] = (features[k].astype(jnp.float32) + mixed).astype(jnp.bfloat16)

    for n in range(len(others)):
        force_copy(n).wait_recv()
    summed = forces[group + mine]
    for n in range(len(others)):
        summed = summed + force_in[n]
    force[...] = summed[:3]

    for n in range(len(links)):
        scal_copy(n).wait_send()
        for h in range(heads):
            value_copy(n, h).wait_send()
    if relay:
        for j in range(group):
            scal_forward(j).wait_send()
            for h in range(heads):
                value_forward(j, h).wait_send()
    for_points(lambda copy: copy.wait_send())
    for n in range(len(partners)):
        for h in range(heads):
            back_copy(n, h).wait_send()
        for c in range(heads // 2):
            finished_copy(n, c).wait_send()
    for n in range(len(others)):
        force_copy(n).wait_send()


def on_device(
    features,
    positions,
    penalty,
    qk_weight,
    value_weight,
    output_weight,
    frames,
    frame_index,
    neighbours,
    counts,
    cotangent,
):
    comp, channels, atoms = features.shape
    ranks = lax.axis_size("head")
    doms = lax.axis_size("dom")
    heads_all = penalty.shape[0]
    group = -(-REACH * BLOCK // atoms)
    heads = heads_all // group
    alpha = qk_weight.shape[1] // (2 * heads_all)
    head_width = channels // heads_all
    per_tile = atoms // BLOCK
    window = 2 * group + 1
    slots = 3 * group
    sent = (comp - 1) * head_width
    rows = sent + 2 * head_width
    others = 3 * group - 1
    links = 2 * group - 1 if ranks == 2 * group else others
    partners = group - 1
    table_rows = len(pair_table(comp))

    framed = frames.transpose(1, 2, 0)
    bf16, f32 = jnp.bfloat16, jnp.float32
    smem = pl.BlockSpec(memory_space=pltpu.SMEM)
    dma = pltpu.SemaphoreType.DMA
    return pl.pallas_call(
        functools.partial(fused_kernel, heads, alpha, doms, ranks, group),
        out_shape=(
            jax.ShapeDtypeStruct(features.shape, bf16),
            jax.ShapeDtypeStruct((positions.shape[0], atoms), f32),
        ),
        in_specs=[smem] * 4 + [pl.BlockSpec(memory_space=pltpu.MemorySpace.HBM)] * 7,
        out_specs=(vmem(), vmem()),
        scratch_shapes=[
            pltpu.VMEM((heads_all, sent, atoms), bf16),
            pltpu.VMEM((slots, heads, rows, atoms), bf16),
            pltpu.VMEM((slots, channels, atoms), bf16),
            pltpu.VMEM((comp, channels, atoms), f32),
            pltpu.VMEM((heads_all, rows, atoms), bf16),
            pltpu.VMEM((group, heads, rows, atoms), bf16),
            pltpu.VMEM((partners, heads // 2, comp, 2 * head_width, atoms), bf16),
            pltpu.VMEM((comp, channels, atoms), bf16),
            pltpu.VMEM((ranks, 8, atoms), f32),
            pltpu.VMEM((slots, 8, atoms), f32),
            pltpu.VMEM((group, atoms, 8), f32),
            pltpu.VMEM((group, table_rows, atoms), f32),
            pltpu.VMEM((group, per_tile, window * atoms), f32),
            pltpu.VMEM((atoms, window * atoms), f32),
            pltpu.VMEM((slots, heads, alpha, atoms), bf16),
            pltpu.VMEM((group, heads, atoms, alpha), bf16),
            pltpu.VMEM((group, 2, rows, atoms), f32),
            pltpu.VMEM((group, heads, atoms, window * atoms), f32),
            pltpu.VMEM((group, heads, atoms, window * atoms), bf16),
            pltpu.VMEM((group, atoms, window * atoms), f32),
            pltpu.VMEM((slots, 8, atoms), f32),
            pltpu.VMEM((others, 8, atoms), f32),
            dma((2, links)),
            dma((2, group)),
            dma((2, links, heads)),
            dma((2, group, heads)),
            dma((2, partners, heads)),
            dma((2, partners, heads // 2)),
            dma((2, others)),
            dma((2, 2)),
            pltpu.VMEM(features.shape, bf16),
            pltpu.VMEM(cotangent.shape, bf16),
            pltpu.VMEM(value_weight.shape, bf16),
            pltpu.VMEM(output_weight.shape, bf16),
            pltpu.VMEM((channels, heads * alpha), bf16),
            pltpu.VMEM((channels, heads * alpha), bf16),
            pltpu.VMEM(framed.shape, f32),
            pltpu.VMEM(positions.shape, f32),
            dma((8,)),
        ],
        compiler_params=pltpu.CompilerParams(
            vmem_limit_bytes=VMEM_LIMIT, collective_id=0, has_side_effects=True
        ),
        name="layer",
    )(
        penalty,
        frame_index,
        neighbours,
        counts,
        features,
        cotangent,
        value_weight,
        output_weight,
        qk_weight,
        framed,
        positions,
    )


def solution(mesh):
    split = ("dom", "head")
    in_specs = (
        P(None, None, split),
        P(None, "dom"),
        P(),
        P(),
        P(),
        P(),
        P(),
        P("dom"),
        P("dom", None),
        P("dom"),
        P(None, None, split),
    )
    out_specs = (P(None, None, split), P(None, split))
    return jax.shard_map(
        on_device, mesh=mesh, in_specs=in_specs, out_specs=out_specs, check_vma=False
    )
```

```python
import functools
import math

import jax
import jax.numpy as jnp
from jax import lax
from jax.experimental import pallas as pl
from jax.experimental.pallas import tpu as pltpu
from jax.sharding import PartitionSpec as P

BLOCK = 64
REACH = 4
FAR = 1e30
VMEM_LIMIT = 63 * 1024 * 1024
PIECES = 5


def degree_of(k):
    return math.isqrt(k)


def pair_table(comp):
    pairs = []
    for k in range(comp):
        l = degree_of(k)
        for m in range(l * l, (l + 1) * (l + 1)):
            pairs.append((k, m))
    return pairs


def vmem():
    return pl.BlockSpec(memory_space=pltpu.VMEM)


def dot(a, b, ca, cb):
    return lax.dot_general(
        a, b, (((ca,), (cb,)), ((), ())), preferred_element_type=jnp.float32
    )


def rotated_rows(coef, tile, comp, source, k, turned):
    index_of = {pair: n for n, pair in enumerate(pair_table(comp))}
    l = degree_of(k)
    total = None
    for m in range(l * l, (l + 1) * (l + 1)):
        row = index_of[(m, k) if turned else (k, m)]
        term = coef[tile, row : row + 1, :] * source(m)
        total = term if total is None else total + term
    return total


def paired(low, high, head_width):
    rows, atoms = low.shape
    shape = (rows // head_width, head_width, atoms)
    return jnp.concatenate([low.reshape(shape), high.reshape(shape)], axis=1).astype(jnp.bfloat16)


def fused_kernel(
    heads,
    alpha,
    doms,
    ranks,
    group,
    penalty,
    frame_index,
    neighbours,
    counts,
    features_in,
    cotangent_in,
    value_weight_in,
    output_weight_in,
    qk_weight_in,
    frames_in,
    positions_in,
    updated,
    force,
    packed,
    vals,
    scal,
    back,
    turned_out,
    turned_in,
    finished,
    arrived,
    own_points,
    points,
    points_t,
    coef,
    mask,
    distance_s,
    keys_s,
    queries_s,
    aggregate_s,
    attention_s,
    rounded_s,
    total_s,
    forces,
    force_in,
    scal_sems,
    scal_forward_sems,
    value_sems,
    forward_sems,
    back_sems,
    finished_sems,
    force_sems,
    point_sems,
    features,
    cotangent,
    value_weight,
    output_weight,
    q_weight,
    k_weight,
    frames,
    positions,
    load_sems,
):
    comp, channels, atoms = features.shape
    head_width = channels // (group * heads)
    half = channels // group
    slots = 3 * group
    window = 2 * group + 1
    per_tile = atoms // BLOCK
    groups = ranks // group
    relay = groups == 2
    sent = (comp - 1) * head_width
    head_columns = heads * alpha
    me = lax.axis_index("head")
    dom = lax.axis_index("dom")
    mine = lax.rem(me, group)
    place = lax.div(me, group)
    up = lax.rem(dom + 1, doms)
    down = lax.rem(dom + doms - 1, doms)

    loads = [
        pltpu.make_async_copy(src, dst, load_sems.at[n])
        for n, (src, dst) in enumerate(
            [
                (features_in, features),
                (value_weight_in, value_weight),
                (positions_in, positions),
                (frames_in, frames),
                (cotangent_in, cotangent),
                (output_weight_in, output_weight),
                (
                    qk_weight_in.at[:, pl.ds(pl.multiple_of(mine * head_columns, 128), head_columns)],
                    q_weight,
                ),
                (
                    qk_weight_in.at[
                        :,
                        pl.ds(
                            pl.multiple_of((group + mine) * head_columns, 128), head_columns
                        ),
                    ],
                    k_weight,
                ),
            ]
        )
    ]
    for load in loads:
        load.start()

    def member(shift):
        return lax.rem(mine + shift, group)

    def group_at(shift):
        at = lax.rem(dom * groups + place + doms * groups + shift, doms * groups)
        return lax.div(at, groups), lax.rem(at, groups)

    others = []
    for shift, base in ((1, 2 * group), (-1, 0)):
        at_dom, at_place = group_at(shift)
        for j in range(group):
            n = member(j)
            others.append(
                (
                    (at_dom, at_place * group + n),
                    n,
                    base + n,
                    2 * group - base + mine,
                    2 * group - base + n,
                )
            )
    partners = []
    for j in range(1, group):
        n = member(j)
        partners.append(((dom, place * group + n), n, group + n, group + mine, group + n))
    others = others + partners

    far = 2 * group * (1 - place)
    near = 2 * group * place
    if relay:
        beside = lax.rem(dom + doms + 1 - 2 * place, doms)
        links = []
        for j in range(group):
            n = member(j)
            links.append(((dom, (1 - place) * group + n), n, far + n, near + mine, far + n))
        links = links + partners
    else:
        links = others

    def remote(src, dst, sems, at, device):
        return pltpu.make_async_remote_copy(
            src_ref=src,
            dst_ref=dst,
            send_sem=sems.at[(0,) + at],
            recv_sem=sems.at[(1,) + at],
            device_id=device,
            device_id_type=pl.DeviceIdType.MESH,
        )

    barrier = pltpu.get_barrier_semaphore()
    greeted = [other[0] for other in others] + [(up, me), (down, me)]
    for device in greeted:
        pl.semaphore_signal(
            barrier, inc=1, device_id=device, device_id_type=pl.DeviceIdType.MESH
        )

    def scal_copy(n):
        device, _, _, there, _ = links[n]
        return remote(scal.at[group + mine], scal.at[there], scal_sems, (n,), device)

    def scal_arrival(n):
        device, _, _, _, here = links[n]
        return remote(scal.at[group + mine], scal.at[here], scal_sems, (n,), device)

    def scal_forward(j):
        n = member(j)
        return remote(
            scal.at[far + n], scal.at[near + n], scal_forward_sems, (j,), (beside, me)
        )

    def value_copy(n, h):
        device, member_there, _, there, _ = links[n]
        return remote(
            packed.at[member_there * heads + h],
            vals.at[there, h, pl.ds(0, sent)],
            value_sems,
            (n, h),
            device,
        )

    def value_arrival(n, h):
        device, member_there, _, _, here = links[n]
        return remote(
            packed.at[member_there * heads + h],
            vals.at[here, h, pl.ds(0, sent)],
            value_sems,
            (n, h),
            device,
        )

    def value_forward(j, h):
        n = member(j)
        return remote(
            vals.at[far + n, h, pl.ds(0, sent)],
            vals.at[near + n, h, pl.ds(0, sent)],
            forward_sems,
            (j, h),
            (beside, me),
        )

    def back_copy(n, h):
        device, member_there, _, _, _ = partners[n]
        return remote(
            turned_out.at[member_there * heads + h], turned_in.at[mine, h], back_sems, (n, h), device
        )

    def back_arrival(n, h):
        device, member_there, _, _, _ = partners[n]
        return remote(
            turned_out.at[member_there * heads + h],
            turned_in.at[member_there, h],
            back_sems,
            (n, h),
            device,
        )

    def finished_rows(of, c):
        return pl.ds(pl.multiple_of(of * half + c * 2 * head_width, 16), 2 * head_width)

    def finished_copy(n, c):
        device, member_there, _, _, _ = partners[n]
        return remote(
            finished.at[n, c], arrived.at[:, finished_rows(mine, c)], finished_sems, (n, c), device
        )

    def finished_arrival(n, c):
        device, member_there, _, _, _ = partners[n]
        return remote(
            finished.at[n, c],
            arrived.at[:, finished_rows(member_there, c)],
            finished_sems,
            (n, c),
            device,
        )

    def force_copy(n):
        device, _, here, _, _ = others[n]
        return remote(forces.at[here], force_in.at[n], force_sems, (n,), device)

    if relay:
        point_copies = [
            (
                None,
                remote(
                    own_points.at[pl.ds((ranks - group) * (1 - place), group)],
                    points.at[pl.ds(near, group)],
                    point_sems,
                    (0,),
                    (beside, me),
                ),
            )
        ]
    else:
        point_copies = [
            (
                place == 0,
                remote(
                    own_points.at[pl.ds(ranks - group, group)],
                    points.at[pl.ds(0, group)],
                    point_sems,
                    (0,),
                    (up, me),
                ),
            ),
            (
                place == groups - 1,
                remote(
                    own_points.at[pl.ds(0, group)],
                    points.at[pl.ds(2 * group, group)],
                    point_sems,
                    (1,),
                    (down, me),
                ),
            ),
        ]

    def for_points(act):
        for holds, copy in point_copies:
            if holds is None:
                act(copy)
            else:
                pl.when(holds)(functools.partial(act, copy))

    for load in loads[:3]:
        load.wait()
    scal[group + mine] = features[0]
    own_points[...] = jnp.zeros_like(own_points)
    for t in range(ranks):
        own_points[t, : positions.shape[0]] = positions[:, t * atoms : (t + 1) * atoms]
    for j in range((comp - 1) // 2):
        low, high = 2 * j + 1, 2 * j + 2
        packed[:, 2 * j * head_width : 2 * (j + 1) * head_width, :] = paired(
            dot(value_weight[degree_of(low)], features[low], 0, 0),
            dot(value_weight[degree_of(high)], features[high], 0, 0),
            head_width,
        )

    pl.semaphore_wait(barrier, len(greeted))

    for n in range(len(links)):
        scal_copy(n).start()
    for_points(lambda copy: copy.start())
    lead = 2
    for h in range(lead):
        for n in range(len(links)):
            value_copy(n, h).start()

    vals[group + mine, :, :sent] = packed[pl.ds(mine * heads, heads)]
    if relay:
        points[pl.ds(group * (1 - place), ranks)] = own_points[...]
    else:
        for s in range(slots):
            t = group * place - group + s

            @pl.when(jnp.logical_and(t >= 0, t < ranks))
            def _():
                points[s] = own_points[t]

    loads[3].wait()
    total_blocks = doms * ranks * per_tile
    lane = lax.broadcasted_iota(jnp.int32, (frames.shape[2], atoms), 1)
    frame_row = lax.broadcasted_iota(jnp.int32, (frames.shape[2], atoms), 0)
    slot_of = lax.broadcasted_iota(jnp.int32, (1, window * atoms), 1) // BLOCK

    def tables(q, carry):
        t = place * group + q
        points_t[q] = own_points[t].T
        wanted = jnp.zeros_like(lane) + frame_index[t * per_tile]
        for r in range(1, per_tile):
            wanted = jnp.where(lane < r * BLOCK, wanted, frame_index[t * per_tile + r])
        onehot = (frame_row == wanted).astype(jnp.float32)
        at = 0
        for l in range(degree_of(comp - 1) + 1):
            first, last = l * l, (l + 1) * (l + 1)
            kept = [
                lax.dot_general(
                    frames[j],
                    onehot,
                    (((1,), (0,)), ((), ())),
                    precision=lax.Precision.HIGHEST,
                    preferred_element_type=jnp.float32,
                )
                for j in range(first, last)
                if abs(j - first - l) <= 2
            ]
            for k in range(first, last):
                rows = None
                for matrix in kept:
                    term = matrix[k : k + 1, :] * matrix[first:last, :]
                    rows = term if rows is None else rows + term
                coef[q, at : at + last - first, :] = rows
                at += last - first
        for r in range(per_tile):
            block = t * per_tile + r
            hidden = jnp.full((1, window * atoms), FAR, jnp.float32)
            shift = r + group * per_tile - REACH
            for s in range(neighbours.shape[1]):
                offset = lax.rem(
                    neighbours[block, s]
                    - (dom * ranks * per_tile + block)
                    + REACH
                    + total_blocks,
                    total_blocks,
                )
                spot = jnp.where(counts[block] > s, offset + shift, -1)
                hidden = jnp.where(slot_of == spot, 0.0, hidden)
            mask[q, r : r + 1, :] = hidden
        return carry

    lax.fori_loop(0, group, tables, 0)

    for load in loads[4:]:
        load.wait()
    for k in range(comp):
        back[k] = (
            dot(output_weight[degree_of(k)], cotangent[k], 1, 0)
            .astype(jnp.bfloat16)
            .astype(jnp.float32)
        )
    strip = 4 * head_width

    def turn(i, carry):
        rows = pl.ds(pl.multiple_of(i * strip, strip), strip)

        def rotated(k):
            return rotated_rows(coef, mine, comp, lambda m: back[m, rows, :], k, True)

        into = pl.ds(i * 4, 4)
        for j in range((comp - 1) // 2):
            turned_out[into, 2 * j * head_width : 2 * (j + 1) * head_width, :] = paired(
                rotated(2 * j + 1), rotated(2 * j + 2), head_width
            )
        first = rotated(0)
        turned_out[into, sent : sent + 2 * head_width, :] = paired(
            first, jnp.zeros_like(first), head_width
        )
        return carry

    lax.fori_loop(0, channels // strip, turn, 0)

    for h in range(lead):
        for n in range(len(partners)):
            back_copy(n, h).start()
    for h in range(lead, heads):
        for n in range(len(links)):
            value_copy(n, h).start()
    for h in range(lead, heads):
        for n in range(len(partners)):
            back_copy(n, h).start()
    turned_in[mine] = turned_out[pl.ds(mine * heads, heads)]

    for n in range(len(links)):
        scal_arrival(n).wait_recv()
    if relay:
        for j in range(group):
            scal_forward(j).start()

    def prepare(slot, carry):
        tile = scal[slot]
        mixed = dot(value_weight[0], tile, 0, 0)
        chosen = mixed[:half]
        for n in range(1, group):
            chosen = jnp.where(mine == n, mixed[n * half : (n + 1) * half], chosen)
        vals[slot, :, sent : sent + 2 * head_width, :] = paired(
            chosen, jnp.zeros_like(chosen), head_width
        )
        keys = dot(k_weight[...], tile, 0, 0)
        keys_s[slot] = keys.reshape(heads, alpha, atoms).astype(jnp.bfloat16)
        return carry

    scale = 1.0 / math.sqrt(alpha)

    def ask(q, carry):
        turned = scal[group + q].astype(jnp.float32).T.astype(jnp.bfloat16)
        for h in range(heads):
            asked = dot(turned, q_weight[:, h * alpha : (h + 1) * alpha], 1, 0)
            queries_s[q, h] = (asked.astype(jnp.bfloat16).astype(jnp.float32) * scale).astype(
                jnp.bfloat16
            )
        return carry

    lax.fori_loop(0, group, ask, 0)
    if relay:
        start = group * (1 - place)
        lax.fori_loop(start, start + 2 * group, prepare, 0)
        for j in range(group):
            scal_forward(j).wait_recv()
        lax.fori_loop(near, near + group, prepare, 0)
    else:
        lax.fori_loop(0, slots, prepare, 0)
    for_points(lambda copy: copy.wait_recv())

    def windowed(q, get):
        return jnp.concatenate([get(q + w) for w in range(window)], axis=-1)

    def attend(q, carry):
        distance = None
        for c in range(3):
            row = windowed(q, lambda s: points[s, c : c + 1, :])
            apart = points_t[q, :, c : c + 1] - row
            distance = apart * apart if distance is None else distance + apart * apart
        hidden = jnp.concatenate(
            [
                jnp.broadcast_to(mask[q, r : r + 1, :], (BLOCK, window * atoms))
                for r in range(per_tile)
            ],
            axis=0,
        )
        distance_s[...] = jnp.maximum(distance, hidden)
        total_s[q] = jnp.zeros_like(distance)

        def head(c, carry):
            for h in (2 * c, 2 * c + 1):
                keys = windowed(q, lambda s: keys_s[s, h])
                strength = penalty[mine * heads + h]
                logits = dot(queries_s[q, h], keys, 1, 0) - strength * distance_s[...]
                peaks = jnp.max(logits, axis=1, keepdims=True)
                exponent = jnp.exp(logits - peaks)
                inverse = 1.0 / jnp.sum(exponent, axis=1, keepdims=True)
                attention = exponent * inverse
                attention_s[q, h] = attention
                rounded_s[q, h] = attention.astype(jnp.bfloat16)
            return carry

        return lax.fori_loop(0, heads // 2, head, carry)

    lax.fori_loop(0, group, attend, 0)

    crossing = len(links) - len(partners)

    def receive(h):
        for n in range(crossing):
            value_arrival(n, h).wait_recv()
        if relay:
            for j in range(group):
                value_forward(j, h).start()

    receive(0)

    def pair(c, carry):
        for part in range(2):
            h = 2 * c + part

            @pl.when(h + 1 < heads)
            def _():
                receive(h + 1)

            if relay:
                for j in range(group):
                    value_forward(j, h).wait_recv()
            for n in range(len(partners)):
                value_arrival(crossing + n, h).wait_recv()
                back_arrival(n, h).wait_recv()

            strength = 2.0 * penalty[mine * heads + h]

            def tile(q, carry):
                values = windowed(q, lambda s: vals[s, h])
                aggregate_s[q, part] = dot(values, rounded_s[q, h], 1, 1)
                turned = turned_in[q, h].astype(jnp.float32).T.astype(jnp.bfloat16)
                weight_grads = dot(turned, values, 1, 0)
                attention = attention_s[q, h]
                weighted = attention * weight_grads
                mean = jnp.sum(weighted, axis=1, keepdims=True)
                total_s[q] = total_s[q] + strength * (weighted - attention * mean)
                return carry

            lax.fori_loop(0, group, tile, 0)

        def rows_of(k):
            return (k - 1) * head_width if k else sent

        def rotated(q, k):
            def source(m):
                at = rows_of(m)
                return jnp.concatenate(
                    [aggregate_s[q, part, at : at + head_width, :] for part in range(2)], axis=0
                )

            return rotated_rows(coef, q, comp, source, k, False).astype(jnp.bfloat16)

        for n in range(len(partners)):
            q = partners[n][1]
            for k in range(comp):
                finished[n, c, k] = rotated(q, k)
            finished_copy(n, c).start()
        for k in range(comp):
            arrived[k, finished_rows(mine, c), :] = rotated(mine, k)
        return carry

    lax.fori_loop(0, heads // 2, pair, 0)

    forces[...] = jnp.zeros_like(forces)
    lane_square = lax.broadcasted_iota(jnp.int32, (atoms, atoms), 1)

    def pull(q, carry):
        total = total_s[q]
        own = jnp.zeros((atoms, atoms), jnp.float32)
        theirs = []
        for c in range(3):
            row = windowed(q, lambda s: points[s, c : c + 1, :])
            weighted = total * (points_t[q, :, c : c + 1] - row)
            own = jnp.where(lane_square == c, jnp.sum(weighted, axis=1, keepdims=True), own)
            theirs.append(jnp.sum(weighted, axis=0, keepdims=True))
        own = own.T
        for c in range(3):
            forces[q + group, c : c + 1, :] = forces[q + group, c : c + 1, :] + own[c : c + 1]
            for w in range(window):
                forces[q + w, c : c + 1, :] = (
                    forces[q + w, c : c + 1, :] - theirs[c][:, w * atoms : (w + 1) * atoms]
                )
        return carry

    lax.fori_loop(0, group, pull, 0)
    for n in range(len(others)):
        force_copy(n).start()

    for n in range(len(links)):
        scal_copy(n).wait_send()
        for h in range(heads):
            value_copy(n, h).wait_send()
    if relay:
        for j in range(group):
            scal_forward(j).wait_send()
            for h in range(heads):
                value_forward(j, h).wait_send()
    for_points(lambda copy: copy.wait_send())
    for n in range(len(partners)):
        for h in range(heads):
            back_copy(n, h).wait_send()
    for n in range(len(partners)):
        for c in range(heads // 2):
            finished_arrival(n, c).wait_recv()
    for k in range(comp):
        mixed = dot(output_weight[degree_of(k)], arrived[k], 0, 0)
        updated[k] = (features[k].astype(jnp.float32) + mixed).astype(jnp.bfloat16)

    for n in range(len(others)):
        force_copy(n).wait_recv()
    summed = forces[group + mine]
    for n in range(len(others)):
        summed = summed + force_in[n]
    force[...] = summed[:3]

    for n in range(len(partners)):
        for c in range(heads // 2):
            finished_copy(n, c).wait_send()
    for n in range(len(others)):
        force_copy(n).wait_send()


def hand_over(pieces, updated_in, force_in, updated, force, sems, held, held_force):
    comp = updated.shape[0]
    fetches, stores = [], []
    for n in range(pieces):
        part = pl.ds(comp * n // pieces, comp * (n + 1) // pieces - comp * n // pieces)
        fetches.append(pltpu.make_async_copy(updated_in.at[part], held.at[part], sems.at[0, n]))
        stores.append(pltpu.make_async_copy(held.at[part], updated.at[part], sems.at[1, n]))
    fetches.append(pltpu.make_async_copy(force_in, held_force, sems.at[0, pieces]))
    stores.append(pltpu.make_async_copy(held_force, force, sems.at[1, pieces]))
    for fetch in fetches:
        fetch.start()
    for fetch, store in zip(fetches, stores):
        fetch.wait()
        store.start()
    for store in stores:
        store.wait()


def on_device(
    features,
    positions,
    penalty,
    qk_weight,
    value_weight,
    output_weight,
    frames,
    frame_index,
    neighbours,
    counts,
    cotangent,
):
    comp, channels, atoms = features.shape
    ranks = lax.axis_size("head")
    doms = lax.axis_size("dom")
    heads_all = penalty.shape[0]
    group = -(-REACH * BLOCK // atoms)
    heads = heads_all // group
    alpha = qk_weight.shape[1] // (2 * heads_all)
    head_width = channels // heads_all
    per_tile = atoms // BLOCK
    window = 2 * group + 1
    slots = 3 * group
    sent = (comp - 1) * head_width
    rows = sent + 2 * head_width
    others = 3 * group - 1
    links = 2 * group - 1 if ranks == 2 * group else others
    partners = group - 1
    table_rows = len(pair_table(comp))

    framed = frames.transpose(1, 2, 0)
    bf16, f32 = jnp.bfloat16, jnp.float32
    smem = pl.BlockSpec(memory_space=pltpu.SMEM)
    dma = pltpu.SemaphoreType.DMA
    updated, force = pl.pallas_call(
        functools.partial(fused_kernel, heads, alpha, doms, ranks, group),
        out_shape=(
            jax.ShapeDtypeStruct(features.shape, bf16),
            jax.ShapeDtypeStruct((positions.shape[0], atoms), f32),
        ),
        in_specs=[smem] * 4 + [pl.BlockSpec(memory_space=pltpu.MemorySpace.HBM)] * 7,
        out_specs=(vmem(), vmem()),
        scratch_shapes=[
            pltpu.VMEM((heads_all, sent, atoms), bf16),
            pltpu.VMEM((slots, heads, rows, atoms), bf16),
            pltpu.VMEM((slots, channels, atoms), bf16),
            pltpu.VMEM((comp, channels, atoms), f32),
            pltpu.VMEM((heads_all, rows, atoms), bf16),
            pltpu.VMEM((group, heads, rows, atoms), bf16),
            pltpu.VMEM((partners, heads // 2, comp, 2 * head_width, atoms), bf16),
            pltpu.VMEM((comp, channels, atoms), bf16),
            pltpu.VMEM((ranks, 8, atoms), f32),
            pltpu.VMEM((slots, 8, atoms), f32),
            pltpu.VMEM((group, atoms, 8), f32),
            pltpu.VMEM((group, table_rows, atoms), f32),
            pltpu.VMEM((group, per_tile, window * atoms), f32),
            pltpu.VMEM((atoms, window * atoms), f32),
            pltpu.VMEM((slots, heads, alpha, atoms), bf16),
            pltpu.VMEM((group, heads, atoms, alpha), bf16),
            pltpu.VMEM((group, 2, rows, atoms), f32),
            pltpu.VMEM((group, heads, atoms, window * atoms), f32),
            pltpu.VMEM((group, heads, atoms, window * atoms), bf16),
            pltpu.VMEM((group, atoms, window * atoms), f32),
            pltpu.VMEM((slots, 8, atoms), f32),
            pltpu.VMEM((others, 8, atoms), f32),
            dma((2, links)),
            dma((2, group)),
            dma((2, links, heads)),
            dma((2, group, heads)),
            dma((2, partners, heads)),
            dma((2, partners, heads // 2)),
            dma((2, others)),
            dma((2, 2)),
            pltpu.VMEM(features.shape, bf16),
            pltpu.VMEM(cotangent.shape, bf16),
            pltpu.VMEM(value_weight.shape, bf16),
            pltpu.VMEM(output_weight.shape, bf16),
            pltpu.VMEM((channels, heads * alpha), bf16),
            pltpu.VMEM((channels, heads * alpha), bf16),
            pltpu.VMEM(framed.shape, f32),
            pltpu.VMEM(positions.shape, f32),
            dma((8,)),
        ],
        compiler_params=pltpu.CompilerParams(
            vmem_limit_bytes=VMEM_LIMIT, collective_id=0, has_side_effects=True
        ),
        name="layer",
    )(
        penalty,
        frame_index,
        neighbours,
        counts,
        features,
        cotangent,
        value_weight,
        output_weight,
        qk_weight,
        framed,
        positions,
    )
    hbm = pl.BlockSpec(memory_space=pltpu.MemorySpace.HBM)
    return pl.pallas_call(
        functools.partial(hand_over, PIECES),
        out_shape=(
            jax.ShapeDtypeStruct(updated.shape, bf16),
            jax.ShapeDtypeStruct(force.shape, f32),
        ),
        in_specs=[hbm, hbm],
        out_specs=(hbm, hbm),
        scratch_shapes=[
            dma((2, PIECES + 1)),
            pltpu.VMEM(updated.shape, bf16),
            pltpu.VMEM(force.shape, f32),
        ],
        name="results",
    )(updated, force)


def solution(mesh):
    split = ("dom", "head")
    in_specs = (
        P(None, None, split),
        P(None, "dom"),
        P(),
        P(),
        P(),
        P(),
        P(),
        P("dom"),
        P("dom", None),
        P("dom"),
        P(None, None, split),
    )
    out_specs = (P(None, None, split), P(None, split))
    return jax.shard_map(
        on_device, mesh=mesh, in_specs=in_specs, out_specs=out_specs, check_vma=False
    )
```

```python
import functools
import math

import jax
import jax.numpy as jnp
from jax import lax
from jax.experimental import pallas as pl
from jax.experimental.pallas import tpu as pltpu
from jax.sharding import PartitionSpec as P

BLOCK = 64
REACH = 4
FAR = 1e30
VMEM_LIMIT = 63 * 1024 * 1024
PIECES = 5


def degree_of(k):
    return math.isqrt(k)


def pair_table(comp):
    pairs = []
    for k in range(comp):
        l = degree_of(k)
        for m in range(l * l, (l + 1) * (l + 1)):
            pairs.append((k, m))
    return pairs


def vmem():
    return pl.BlockSpec(memory_space=pltpu.VMEM)


def dot(a, b, ca, cb):
    return lax.dot_general(
        a, b, (((ca,), (cb,)), ((), ())), preferred_element_type=jnp.float32
    )


def rotated_rows(coef, tile, comp, source, k, turned):
    index_of = {pair: n for n, pair in enumerate(pair_table(comp))}
    l = degree_of(k)
    total = None
    for m in range(l * l, (l + 1) * (l + 1)):
        row = index_of[(m, k) if turned else (k, m)]
        term = coef[tile, row : row + 1, :] * source(m)
        total = term if total is None else total + term
    return total


def paired(low, high, head_width):
    rows, atoms = low.shape
    shape = (rows // head_width, head_width, atoms)
    return jnp.concatenate([low.reshape(shape), high.reshape(shape)], axis=1).astype(jnp.bfloat16)


def fused_kernel(
    heads,
    alpha,
    doms,
    ranks,
    group,
    penalty,
    frame_index,
    neighbours,
    counts,
    features_in,
    cotangent_in,
    value_weight_in,
    output_weight_in,
    qk_weight_in,
    frames_in,
    positions_in,
    updated,
    force,
    packed,
    vals,
    scal,
    back,
    turned_out,
    turned_in,
    finished,
    arrived,
    own_points,
    points,
    points_t,
    coef,
    mask,
    distance_s,
    keys_s,
    queries_s,
    aggregate_s,
    attention_s,
    rounded_s,
    total_s,
    forces,
    force_in,
    scal_sems,
    scal_forward_sems,
    value_sems,
    forward_sems,
    back_sems,
    finished_sems,
    force_sems,
    point_sems,
    features,
    cotangent,
    value_weight,
    output_weight,
    q_weight,
    k_weight,
    frames,
    positions,
    load_sems,
):
    comp, channels, atoms = features.shape
    head_width = channels // (group * heads)
    half = channels // group
    slots = 3 * group
    window = 2 * group + 1
    per_tile = atoms // BLOCK
    groups = ranks // group
    relay = groups == 2
    sent = (comp - 1) * head_width
    head_columns = heads * alpha
    me = lax.axis_index("head")
    dom = lax.axis_index("dom")
    mine = lax.rem(me, group)
    place = lax.div(me, group)
    up = lax.rem(dom + 1, doms)
    down = lax.rem(dom + doms - 1, doms)

    loads = [
        pltpu.make_async_copy(src, dst, load_sems.at[n])
        for n, (src, dst) in enumerate(
            [
                (features_in, features),
                (value_weight_in, value_weight),
                (positions_in, positions),
                (frames_in, frames),
                (cotangent_in, cotangent),
                (output_weight_in, output_weight),
                (
                    qk_weight_in.at[:, pl.ds(pl.multiple_of(mine * head_columns, 128), head_columns)],
                    q_weight,
                ),
                (
                    qk_weight_in.at[
                        :,
                        pl.ds(
                            pl.multiple_of((group + mine) * head_columns, 128), head_columns
                        ),
                    ],
                    k_weight,
                ),
            ]
        )
    ]
    for load in loads:
        load.start()

    def member(shift):
        return lax.rem(mine + shift, group)

    def group_at(shift):
        at = lax.rem(dom * groups + place + doms * groups + shift, doms * groups)
        return lax.div(at, groups), lax.rem(at, groups)

    others = []
    for shift, base in ((1, 2 * group), (-1, 0)):
        at_dom, at_place = group_at(shift)
        for j in range(group):
            n = member(j)
            others.append(
                (
                    (at_dom, at_place * group + n),
                    n,
                    base + n,
                    2 * group - base + mine,
                    2 * group - base + n,
                )
            )
    partners = []
    for j in range(1, group):
        n = member(j)
        partners.append(((dom, place * group + n), n, group + n, group + mine, group + n))
    others = others + partners

    far = 2 * group * (1 - place)
    near = 2 * group * place
    if relay:
        beside = lax.rem(dom + doms + 1 - 2 * place, doms)
        links = []
        for j in range(group):
            n = member(j)
            links.append(((dom, (1 - place) * group + n), n, far + n, near + mine, far + n))
        links = links + partners
    else:
        links = others

    def remote(src, dst, sems, at, device):
        return pltpu.make_async_remote_copy(
            src_ref=src,
            dst_ref=dst,
            send_sem=sems.at[(0,) + at],
            recv_sem=sems.at[(1,) + at],
            device_id=device,
            device_id_type=pl.DeviceIdType.MESH,
        )

    barrier = pltpu.get_barrier_semaphore()
    greeted = [other[0] for other in others] + [(up, me), (down, me)]
    for device in greeted:
        pl.semaphore_signal(
            barrier, inc=1, device_id=device, device_id_type=pl.DeviceIdType.MESH
        )

    def scal_copy(n):
        device, _, _, there, _ = links[n]
        return remote(scal.at[group + mine], scal.at[there], scal_sems, (n,), device)

    def scal_arrival(n):
        device, _, _, _, here = links[n]
        return remote(scal.at[group + mine], scal.at[here], scal_sems, (n,), device)

    def scal_forward(j):
        n = member(j)
        return remote(
            scal.at[far + n], scal.at[near + n], scal_forward_sems, (j,), (beside, me)
        )

    def value_copy(n, h):
        device, member_there, _, there, _ = links[n]
        return remote(
            packed.at[member_there * heads + h],
            vals.at[there, h, pl.ds(0, sent)],
            value_sems,
            (n, h),
            device,
        )

    def value_arrival(n, h):
        device, member_there, _, _, here = links[n]
        return remote(
            packed.at[member_there * heads + h],
            vals.at[here, h, pl.ds(0, sent)],
            value_sems,
            (n, h),
            device,
        )

    def value_forward(j, h):
        n = member(j)
        return remote(
            vals.at[far + n, h, pl.ds(0, sent)],
            vals.at[near + n, h, pl.ds(0, sent)],
            forward_sems,
            (j, h),
            (beside, me),
        )

    def back_copy(n, h):
        device, member_there, _, _, _ = partners[n]
        return remote(
            turned_out.at[member_there * heads + h], turned_in.at[mine, h], back_sems, (n, h), device
        )

    def back_arrival(n, h):
        device, member_there, _, _, _ = partners[n]
        return remote(
            turned_out.at[member_there * heads + h],
            turned_in.at[member_there, h],
            back_sems,
            (n, h),
            device,
        )

    def finished_rows(of, c):
        return pl.ds(pl.multiple_of(of * half + c * 2 * head_width, 16), 2 * head_width)

    def finished_copy(n, c):
        device, member_there, _, _, _ = partners[n]
        return remote(
            finished.at[n, c], arrived.at[:, finished_rows(mine, c)], finished_sems, (n, c), device
        )

    def finished_arrival(n, c):
        device, member_there, _, _, _ = partners[n]
        return remote(
            finished.at[n, c],
            arrived.at[:, finished_rows(member_there, c)],
            finished_sems,
            (n, c),
            device,
        )

    def force_copy(n):
        device, _, here, _, _ = others[n]
        return remote(forces.at[here], force_in.at[n], force_sems, (n,), device)

    if relay:
        point_copies = [
            (
                None,
                remote(
                    own_points.at[pl.ds((ranks - group) * (1 - place), group)],
                    points.at[pl.ds(near, group)],
                    point_sems,
                    (0,),
                    (beside, me),
                ),
            )
        ]
    else:
        point_copies = [
            (
                place == 0,
                remote(
                    own_points.at[pl.ds(ranks - group, group)],
                    points.at[pl.ds(0, group)],
                    point_sems,
                    (0,),
                    (up, me),
                ),
            ),
            (
                place == groups - 1,
                remote(
                    own_points.at[pl.ds(0, group)],
                    points.at[pl.ds(2 * group, group)],
                    point_sems,
                    (1,),
                    (down, me),
                ),
            ),
        ]

    def for_points(act):
        for holds, copy in point_copies:
            if holds is None:
                act(copy)
            else:
                pl.when(holds)(functools.partial(act, copy))

    for load in loads[:3]:
        load.wait()
    scal[group + mine] = features[0]
    own_points[...] = jnp.zeros_like(own_points)
    for t in range(ranks):
        own_points[t, : positions.shape[0]] = positions[:, t * atoms : (t + 1) * atoms]
    for j in range((comp - 1) // 2):
        low, high = 2 * j + 1, 2 * j + 2
        packed[:, 2 * j * head_width : 2 * (j + 1) * head_width, :] = paired(
            dot(value_weight[degree_of(low)], features[low], 0, 0),
            dot(value_weight[degree_of(high)], features[high], 0, 0),
            head_width,
        )

    pl.semaphore_wait(barrier, len(greeted))

    for n in range(len(links)):
        scal_copy(n).start()
    for_points(lambda copy: copy.start())
    lead = 2
    for h in range(lead):
        for n in range(len(links)):
            value_copy(n, h).start()

    vals[group + mine, :, :sent] = packed[pl.ds(mine * heads, heads)]
    if relay:
        points[pl.ds(group * (1 - place), ranks)] = own_points[...]
    else:
        for s in range(slots):
            t = group * place - group + s

            @pl.when(jnp.logical_and(t >= 0, t < ranks))
            def _():
                points[s] = own_points[t]

    loads[3].wait()
    total_blocks = doms * ranks * per_tile
    lane = lax.broadcasted_iota(jnp.int32, (frames.shape[2], atoms), 1)
    frame_row = lax.broadcasted_iota(jnp.int32, (frames.shape[2], atoms), 0)
    slot_of = lax.broadcasted_iota(jnp.int32, (1, window * atoms), 1) // BLOCK

    def tables(q, carry):
        t = place * group + q
        points_t[q] = own_points[t].T
        wanted = jnp.zeros_like(lane) + frame_index[t * per_tile]
        for r in range(1, per_tile):
            wanted = jnp.where(lane < r * BLOCK, wanted, frame_index[t * per_tile + r])
        onehot = (frame_row == wanted).astype(jnp.float32)
        at = 0
        for l in range(degree_of(comp - 1) + 1):
            first, last = l * l, (l + 1) * (l + 1)
            kept = [
                lax.dot_general(
                    frames[j],
                    onehot,
                    (((1,), (0,)), ((), ())),
                    precision=lax.Precision.HIGHEST,
                    preferred_element_type=jnp.float32,
                )
                for j in range(first, last)
                if abs(j - first - l) <= 2
            ]
            for k in range(first, last):
                rows = None
                for matrix in kept:
                    term = matrix[k : k + 1, :] * matrix[first:last, :]
                    rows = term if rows is None else rows + term
                coef[q, at : at + last - first, :] = rows
                at += last - first
        for r in range(per_tile):
            block = t * per_tile + r
            hidden = jnp.full((1, window * atoms), FAR, jnp.float32)
            shift = r + group * per_tile - REACH
            for s in range(neighbours.shape[1]):
                offset = lax.rem(
                    neighbours[block, s]
                    - (dom * ranks * per_tile + block)
                    + REACH
                    + total_blocks,
                    total_blocks,
                )
                spot = jnp.where(counts[block] > s, offset + shift, -1)
                hidden = jnp.where(slot_of == spot, 0.0, hidden)
            mask[q, r : r + 1, :] = hidden
        return carry

    lax.fori_loop(0, group, tables, 0)

    for load in loads[4:]:
        load.wait()
    for k in range(comp):
        back[k] = (
            dot(output_weight[degree_of(k)], cotangent[k], 1, 0)
            .astype(jnp.bfloat16)
            .astype(jnp.float32)
        )
    strip = 4 * head_width

    def turn(i, carry):
        rows = pl.ds(pl.multiple_of(i * strip, strip), strip)

        def rotated(k):
            return rotated_rows(coef, mine, comp, lambda m: back[m, rows, :], k, True)

        into = pl.ds(i * 4, 4)
        for j in range((comp - 1) // 2):
            turned_out[into, 2 * j * head_width : 2 * (j + 1) * head_width, :] = paired(
                rotated(2 * j + 1), rotated(2 * j + 2), head_width
            )
        first = rotated(0)
        turned_out[into, sent : sent + 2 * head_width, :] = paired(
            first, jnp.zeros_like(first), head_width
        )
        return carry

    lax.fori_loop(0, channels // strip, turn, 0)

    for h in range(lead):
        for n in range(len(partners)):
            back_copy(n, h).start()
    for h in range(lead, heads):
        for n in range(len(links)):
            value_copy(n, h).start()
    for h in range(lead, heads):
        for n in range(len(partners)):
            back_copy(n, h).start()
    turned_in[mine] = turned_out[pl.ds(mine * heads, heads)]

    for n in range(len(links)):
        scal_arrival(n).wait_recv()
    if relay:
        for j in range(group):
            scal_forward(j).start()

    def prepare(slot, carry):
        tile = scal[slot]
        mixed = dot(value_weight[0], tile, 0, 0)
        chosen = mixed[:half]
        for n in range(1, group):
            chosen = jnp.where(mine == n, mixed[n * half : (n + 1) * half], chosen)
        vals[slot, :, sent : sent + 2 * head_width, :] = paired(
            chosen, jnp.zeros_like(chosen), head_width
        )
        keys = dot(k_weight[...], tile, 0, 0)
        keys_s[slot] = keys.reshape(heads, alpha, atoms).astype(jnp.bfloat16)
        return carry

    scale = 1.0 / math.sqrt(alpha)

    def ask(q, carry):
        turned = scal[group + q].astype(jnp.float32).T.astype(jnp.bfloat16)
        for h in range(heads):
            asked = dot(turned, q_weight[:, h * alpha : (h + 1) * alpha], 1, 0)
            queries_s[q, h] = (asked.astype(jnp.bfloat16).astype(jnp.float32) * scale).astype(
                jnp.bfloat16
            )
        return carry

    lax.fori_loop(0, group, ask, 0)
    if relay:
        start = group * (1 - place)
        lax.fori_loop(start, start + 2 * group, prepare, 0)
        for j in range(group):
            scal_forward(j).wait_recv()
        lax.fori_loop(near, near + group, prepare, 0)
    else:
        lax.fori_loop(0, slots, prepare, 0)
    for_points(lambda copy: copy.wait_recv())

    def windowed(q, get):
        return jnp.concatenate([get(q + w) for w in range(window)], axis=-1)

    def attend(q, carry):
        distance = None
        for c in range(3):
            row = windowed(q, lambda s: points[s, c : c + 1, :])
            apart = points_t[q, :, c : c + 1] - row
            distance = apart * apart if distance is None else distance + apart * apart
        hidden = jnp.concatenate(
            [
                jnp.broadcast_to(mask[q, r : r + 1, :], (BLOCK, window * atoms))
                for r in range(per_tile)
            ],
            axis=0,
        )
        distance_s[...] = jnp.maximum(distance, hidden)
        total_s[q] = jnp.zeros_like(distance)

        def head(c, carry):
            for h in (2 * c, 2 * c + 1):
                keys = windowed(q, lambda s: keys_s[s, h])
                strength = penalty[mine * heads + h]
                logits = dot(queries_s[q, h], keys, 1, 0) - strength * distance_s[...]
                peaks = jnp.max(logits, axis=1, keepdims=True)
                exponent = jnp.exp(logits - peaks)
                inverse = 1.0 / jnp.sum(exponent, axis=1, keepdims=True)
                attention = exponent * inverse
                attention_s[q, h] = attention
                rounded_s[q, h] = attention.astype(jnp.bfloat16)
            return carry

        return lax.fori_loop(0, heads // 2, head, carry)

    lax.fori_loop(0, group, attend, 0)

    crossing = len(links) - len(partners)

    def receive(h):
        for n in range(crossing):
            value_arrival(n, h).wait_recv()
        if relay:
            for j in range(group):
                value_forward(j, h).start()

    receive(0)

    last = heads // 2 - 1

    def finish(c):
        def rows_of(k):
            return (k - 1) * head_width if k else sent

        def rotated(q, k):
            def source(m):
                at = rows_of(m)
                return jnp.concatenate(
                    [aggregate_s[q, part, at : at + head_width, :] for part in range(2)], axis=0
                )

            return rotated_rows(coef, q, comp, source, k, False).astype(jnp.bfloat16)

        for n in range(len(partners)):
            q = partners[n][1]
            for k in range(comp):
                finished[n, c, k] = rotated(q, k)
            finished_copy(n, c).start()
        for k in range(comp):
            arrived[k, finished_rows(mine, c), :] = rotated(mine, k)

    def pair(c, carry):
        for part in range(2):
            h = 2 * c + part

            @pl.when(h + 1 < heads)
            def _():
                receive(h + 1)

            if relay:
                for j in range(group):
                    value_forward(j, h).wait_recv()
            for n in range(len(partners)):
                value_arrival(crossing + n, h).wait_recv()
                back_arrival(n, h).wait_recv()

            strength = 2.0 * penalty[mine * heads + h]

            def tile(q, carry):
                values = windowed(q, lambda s: vals[s, h])
                aggregate_s[q, part] = dot(values, rounded_s[q, h], 1, 1)
                turned = turned_in[q, h].astype(jnp.float32).T.astype(jnp.bfloat16)
                weight_grads = dot(turned, values, 1, 0)
                attention = attention_s[q, h]
                weighted = attention * weight_grads
                mean = jnp.sum(weighted, axis=1, keepdims=True)
                total_s[q] = total_s[q] + strength * (weighted - attention * mean)
                return carry

            lax.fori_loop(0, group, tile, 0)

        pl.when(c < last)(lambda: finish(c))
        return carry

    lax.fori_loop(0, heads // 2, pair, 0)

    forces[...] = jnp.zeros_like(forces)
    lane_square = lax.broadcasted_iota(jnp.int32, (atoms, atoms), 1)

    def pull(q, carry):
        total = total_s[q]
        own = jnp.zeros((atoms, atoms), jnp.float32)
        theirs = []
        for c in range(3):
            row = windowed(q, lambda s: points[s, c : c + 1, :])
            weighted = total * (points_t[q, :, c : c + 1] - row)
            own = jnp.where(lane_square == c, jnp.sum(weighted, axis=1, keepdims=True), own)
            theirs.append(jnp.sum(weighted, axis=0, keepdims=True))
        own = own.T
        for c in range(3):
            forces[q + group, c : c + 1, :] = forces[q + group, c : c + 1, :] + own[c : c + 1]
            for w in range(window):
                forces[q + w, c : c + 1, :] = (
                    forces[q + w, c : c + 1, :] - theirs[c][:, w * atoms : (w + 1) * atoms]
                )
        return carry

    lax.fori_loop(0, group, pull, 0)
    for n in range(len(others)):
        force_copy(n).start()
    finish(last)

    for n in range(len(links)):
        scal_copy(n).wait_send()
        for h in range(heads):
            value_copy(n, h).wait_send()
    if relay:
        for j in range(group):
            scal_forward(j).wait_send()
            for h in range(heads):
                value_forward(j, h).wait_send()
    for_points(lambda copy: copy.wait_send())
    for n in range(len(partners)):
        for h in range(heads):
            back_copy(n, h).wait_send()
    for n in range(len(partners)):
        for c in range(heads // 2):
            finished_arrival(n, c).wait_recv()
    for k in range(comp):
        mixed = dot(output_weight[degree_of(k)], arrived[k], 0, 0)
        updated[k] = (features[k].astype(jnp.float32) + mixed).astype(jnp.bfloat16)

    for n in range(len(others)):
        force_copy(n).wait_recv()
    summed = forces[group + mine]
    for n in range(len(others)):
        summed = summed + force_in[n]
    force[...] = summed[:3]

    for n in range(len(partners)):
        for c in range(heads // 2):
            finished_copy(n, c).wait_send()
    for n in range(len(others)):
        force_copy(n).wait_send()


def hand_over(pieces, updated_in, force_in, updated, force, sems, held, held_force):
    comp = updated.shape[0]
    fetches, stores = [], []
    for n in range(pieces):
        part = pl.ds(comp * n // pieces, comp * (n + 1) // pieces - comp * n // pieces)
        fetches.append(pltpu.make_async_copy(updated_in.at[part], held.at[part], sems.at[0, n]))
        stores.append(pltpu.make_async_copy(held.at[part], updated.at[part], sems.at[1, n]))
    fetches.append(pltpu.make_async_copy(force_in, held_force, sems.at[0, pieces]))
    stores.append(pltpu.make_async_copy(held_force, force, sems.at[1, pieces]))
    for fetch in fetches:
        fetch.start()
    for fetch, store in zip(fetches, stores):
        fetch.wait()
        store.start()
    for store in stores:
        store.wait()


def on_device(
    features,
    positions,
    penalty,
    qk_weight,
    value_weight,
    output_weight,
    frames,
    frame_index,
    neighbours,
    counts,
    cotangent,
):
    comp, channels, atoms = features.shape
    ranks = lax.axis_size("head")
    doms = lax.axis_size("dom")
    heads_all = penalty.shape[0]
    group = -(-REACH * BLOCK // atoms)
    heads = heads_all // group
    alpha = qk_weight.shape[1] // (2 * heads_all)
    head_width = channels // heads_all
    per_tile = atoms // BLOCK
    window = 2 * group + 1
    slots = 3 * group
    sent = (comp - 1) * head_width
    rows = sent + 2 * head_width
    others = 3 * group - 1
    links = 2 * group - 1 if ranks == 2 * group else others
    partners = group - 1
    table_rows = len(pair_table(comp))

    framed = frames.transpose(1, 2, 0)
    bf16, f32 = jnp.bfloat16, jnp.float32
    smem = pl.BlockSpec(memory_space=pltpu.SMEM)
    dma = pltpu.SemaphoreType.DMA
    updated, force = pl.pallas_call(
        functools.partial(fused_kernel, heads, alpha, doms, ranks, group),
        out_shape=(
            jax.ShapeDtypeStruct(features.shape, bf16),
            jax.ShapeDtypeStruct((positions.shape[0], atoms), f32),
        ),
        in_specs=[smem] * 4 + [pl.BlockSpec(memory_space=pltpu.MemorySpace.HBM)] * 7,
        out_specs=(vmem(), vmem()),
        scratch_shapes=[
            pltpu.VMEM((heads_all, sent, atoms), bf16),
            pltpu.VMEM((slots, heads, rows, atoms), bf16),
            pltpu.VMEM((slots, channels, atoms), bf16),
            pltpu.VMEM((comp, channels, atoms), f32),
            pltpu.VMEM((heads_all, rows, atoms), bf16),
            pltpu.VMEM((group, heads, rows, atoms), bf16),
            pltpu.VMEM((partners, heads // 2, comp, 2 * head_width, atoms), bf16),
            pltpu.VMEM((comp, channels, atoms), bf16),
            pltpu.VMEM((ranks, 8, atoms), f32),
            pltpu.VMEM((slots, 8, atoms), f32),
            pltpu.VMEM((group, atoms, 8), f32),
            pltpu.VMEM((group, table_rows, atoms), f32),
            pltpu.VMEM((group, per_tile, window * atoms), f32),
            pltpu.VMEM((atoms, window * atoms), f32),
            pltpu.VMEM((slots, heads, alpha, atoms), bf16),
            pltpu.VMEM((group, heads, atoms, alpha), bf16),
            pltpu.VMEM((group, 2, rows, atoms), f32),
            pltpu.VMEM((group, heads, atoms, window * atoms), f32),
            pltpu.VMEM((group, heads, atoms, window * atoms), bf16),
            pltpu.VMEM((group, atoms, window * atoms), f32),
            pltpu.VMEM((slots, 8, atoms), f32),
            pltpu.VMEM((others, 8, atoms), f32),
            dma((2, links)),
            dma((2, group)),
            dma((2, links, heads)),
            dma((2, group, heads)),
            dma((2, partners, heads)),
            dma((2, partners, heads // 2)),
            dma((2, others)),
            dma((2, 2)),
            pltpu.VMEM(features.shape, bf16),
            pltpu.VMEM(cotangent.shape, bf16),
            pltpu.VMEM(value_weight.shape, bf16),
            pltpu.VMEM(output_weight.shape, bf16),
            pltpu.VMEM((channels, heads * alpha), bf16),
            pltpu.VMEM((channels, heads * alpha), bf16),
            pltpu.VMEM(framed.shape, f32),
            pltpu.VMEM(positions.shape, f32),
            dma((8,)),
        ],
        compiler_params=pltpu.CompilerParams(
            vmem_limit_bytes=VMEM_LIMIT, collective_id=0, has_side_effects=True
        ),
        name="layer",
    )(
        penalty,
        frame_index,
        neighbours,
        counts,
        features,
        cotangent,
        value_weight,
        output_weight,
        qk_weight,
        framed,
        positions,
    )
    hbm = pl.BlockSpec(memory_space=pltpu.MemorySpace.HBM)
    return pl.pallas_call(
        functools.partial(hand_over, PIECES),
        out_shape=(
            jax.ShapeDtypeStruct(updated.shape, bf16),
            jax.ShapeDtypeStruct(force.shape, f32),
        ),
        in_specs=[hbm, hbm],
        out_specs=(hbm, hbm),
        scratch_shapes=[
            dma((2, PIECES + 1)),
            pltpu.VMEM(updated.shape, bf16),
            pltpu.VMEM(force.shape, f32),
        ],
        name="results",
    )(updated, force)


def solution(mesh):
    split = ("dom", "head")
    in_specs = (
        P(None, None, split),
        P(None, "dom"),
        P(),
        P(),
        P(),
        P(),
        P(),
        P("dom"),
        P("dom", None),
        P("dom"),
        P(None, None, split),
    )
    out_specs = (P(None, None, split), P(None, split))
    return jax.shard_map(
        on_device, mesh=mesh, in_specs=in_specs, out_specs=out_specs, check_vma=False
    )
```

```python
import functools
import math

import jax
import jax.numpy as jnp
from jax import lax
from jax.experimental import pallas as pl
from jax.experimental.pallas import tpu as pltpu
from jax.sharding import PartitionSpec as P

BLOCK = 64
REACH = 4
FAR = 1e30
VMEM_LIMIT = 63 * 1024 * 1024
PIECES = 5


def degree_of(k):
    return math.isqrt(k)


def pair_table(comp):
    pairs = []
    for k in range(comp):
        l = degree_of(k)
        for m in range(l * l, (l + 1) * (l + 1)):
            pairs.append((k, m))
    return pairs


def vmem():
    return pl.BlockSpec(memory_space=pltpu.VMEM)


def dot(a, b, ca, cb):
    return lax.dot_general(
        a, b, (((ca,), (cb,)), ((), ())), preferred_element_type=jnp.float32
    )


def rotated_rows(coef, tile, comp, source, k, turned):
    index_of = {pair: n for n, pair in enumerate(pair_table(comp))}
    l = degree_of(k)
    total = None
    for m in range(l * l, (l + 1) * (l + 1)):
        row = index_of[(m, k) if turned else (k, m)]
        term = coef[tile, row : row + 1, :] * source(m)
        total = term if total is None else total + term
    return total


def paired(low, high, head_width):
    rows, atoms = low.shape
    shape = (rows // head_width, head_width, atoms)
    return jnp.concatenate([low.reshape(shape), high.reshape(shape)], axis=1).astype(jnp.bfloat16)


def fused_kernel(
    heads,
    alpha,
    doms,
    ranks,
    group,
    penalty,
    frame_index,
    neighbours,
    counts,
    features_in,
    cotangent_in,
    value_weight_in,
    output_weight_in,
    qk_weight_in,
    frames_in,
    positions_in,
    updated,
    force,
    packed,
    vals,
    scal,
    back,
    turned_out,
    turned_in,
    finished,
    arrived,
    own_points,
    points,
    points_t,
    coef,
    mask,
    distance_s,
    keys_s,
    queries_s,
    aggregate_s,
    attention_s,
    rounded_s,
    total_s,
    forces,
    force_in,
    scal_sems,
    scal_forward_sems,
    value_sems,
    forward_sems,
    back_sems,
    finished_sems,
    force_sems,
    point_sems,
    features,
    cotangent,
    value_weight,
    output_weight,
    q_weight,
    k_weight,
    frames,
    positions,
    load_sems,
):
    comp, channels, atoms = features.shape
    head_width = channels // (group * heads)
    half = channels // group
    slots = 3 * group
    window = 2 * group + 1
    per_tile = atoms // BLOCK
    groups = ranks // group
    relay = groups == 2
    sent = (comp - 1) * head_width
    head_columns = heads * alpha
    me = lax.axis_index("head")
    dom = lax.axis_index("dom")
    mine = lax.rem(me, group)
    place = lax.div(me, group)
    up = lax.rem(dom + 1, doms)
    down = lax.rem(dom + doms - 1, doms)

    loads = [
        pltpu.make_async_copy(src, dst, load_sems.at[n])
        for n, (src, dst) in enumerate(
            [
                (features_in, features),
                (value_weight_in, value_weight),
                (positions_in, positions),
                (frames_in, frames),
                (cotangent_in, cotangent),
                (output_weight_in, output_weight),
                (
                    qk_weight_in.at[:, pl.ds(pl.multiple_of(mine * head_columns, 128), head_columns)],
                    q_weight,
                ),
                (
                    qk_weight_in.at[
                        :,
                        pl.ds(
                            pl.multiple_of((group + mine) * head_columns, 128), head_columns
                        ),
                    ],
                    k_weight,
                ),
            ]
        )
    ]
    for load in loads:
        load.start()

    def member(shift):
        return lax.rem(mine + shift, group)

    def group_at(shift):
        at = lax.rem(dom * groups + place + doms * groups + shift, doms * groups)
        return lax.div(at, groups), lax.rem(at, groups)

    others = []
    for shift, base in ((1, 2 * group), (-1, 0)):
        at_dom, at_place = group_at(shift)
        for j in range(group):
            n = member(j)
            others.append(
                (
                    (at_dom, at_place * group + n),
                    n,
                    base + n,
                    2 * group - base + mine,
                    2 * group - base + n,
                )
            )
    partners = []
    for j in range(1, group):
        n = member(j)
        partners.append(((dom, place * group + n), n, group + n, group + mine, group + n))
    others = others + partners

    far = 2 * group * (1 - place)
    near = 2 * group * place
    if relay:
        beside = lax.rem(dom + doms + 1 - 2 * place, doms)
        links = []
        for j in range(group):
            n = member(j)
            links.append(((dom, (1 - place) * group + n), n, far + n, near + mine, far + n))
        links = links + partners
    else:
        links = others

    def remote(src, dst, sems, at, device):
        return pltpu.make_async_remote_copy(
            src_ref=src,
            dst_ref=dst,
            send_sem=sems.at[(0,) + at],
            recv_sem=sems.at[(1,) + at],
            device_id=device,
            device_id_type=pl.DeviceIdType.MESH,
        )

    barrier = pltpu.get_barrier_semaphore()
    greeted = [other[0] for other in others] + [(up, me), (down, me)]
    for device in greeted:
        pl.semaphore_signal(
            barrier, inc=1, device_id=device, device_id_type=pl.DeviceIdType.MESH
        )

    def scal_copy(n):
        device, _, _, there, _ = links[n]
        return remote(scal.at[group + mine], scal.at[there], scal_sems, (n,), device)

    def scal_arrival(n):
        device, _, _, _, here = links[n]
        return remote(scal.at[group + mine], scal.at[here], scal_sems, (n,), device)

    def scal_forward(j):
        n = member(j)
        return remote(
            scal.at[far + n], scal.at[near + n], scal_forward_sems, (j,), (beside, me)
        )

    def value_copy(n, h):
        device, member_there, _, there, _ = links[n]
        return remote(
            packed.at[member_there * heads + h],
            vals.at[there, h, pl.ds(0, sent)],
            value_sems,
            (n, h),
            device,
        )

    def value_arrival(n, h):
        device, member_there, _, _, here = links[n]
        return remote(
            packed.at[member_there * heads + h],
            vals.at[here, h, pl.ds(0, sent)],
            value_sems,
            (n, h),
            device,
        )

    def value_forward(j, h):
        n = member(j)
        return remote(
            vals.at[far + n, h, pl.ds(0, sent)],
            vals.at[near + n, h, pl.ds(0, sent)],
            forward_sems,
            (j, h),
            (beside, me),
        )

    def back_copy(n, h):
        device, member_there, _, _, _ = partners[n]
        return remote(
            turned_out.at[member_there * heads + h], turned_in.at[mine, h], back_sems, (n, h), device
        )

    def back_arrival(n, h):
        device, member_there, _, _, _ = partners[n]
        return remote(
            turned_out.at[member_there * heads + h],
            turned_in.at[member_there, h],
            back_sems,
            (n, h),
            device,
        )

    def finished_rows(of, c):
        return pl.ds(pl.multiple_of(of * half + c * 2 * head_width, 16), 2 * head_width)

    def finished_copy(n, c):
        device, member_there, _, _, _ = partners[n]
        return remote(
            finished.at[n, c], arrived.at[:, finished_rows(mine, c)], finished_sems, (n, c), device
        )

    def finished_arrival(n, c):
        device, member_there, _, _, _ = partners[n]
        return remote(
            finished.at[n, c],
            arrived.at[:, finished_rows(member_there, c)],
            finished_sems,
            (n, c),
            device,
        )

    def force_copy(n):
        device, _, here, _, _ = others[n]
        return remote(forces.at[here], force_in.at[n], force_sems, (n,), device)

    if relay:
        point_copies = [
            (
                None,
                remote(
                    own_points.at[pl.ds((ranks - group) * (1 - place), group)],
                    points.at[pl.ds(near, group)],
                    point_sems,
                    (0,),
                    (beside, me),
                ),
            )
        ]
    else:
        point_copies = [
            (
                place == 0,
                remote(
                    own_points.at[pl.ds(ranks - group, group)],
                    points.at[pl.ds(0, group)],
                    point_sems,
                    (0,),
                    (up, me),
                ),
            ),
            (
                place == groups - 1,
                remote(
                    own_points.at[pl.ds(0, group)],
                    points.at[pl.ds(2 * group, group)],
                    point_sems,
                    (1,),
                    (down, me),
                ),
            ),
        ]

    def for_points(act):
        for holds, copy in point_copies:
            if holds is None:
                act(copy)
            else:
                pl.when(holds)(functools.partial(act, copy))

    for load in loads[:3]:
        load.wait()
    scal[group + mine] = features[0]
    own_points[...] = jnp.zeros_like(own_points)
    for t in range(ranks):
        own_points[t, : positions.shape[0]] = positions[:, t * atoms : (t + 1) * atoms]
    for j in range((comp - 1) // 2):
        low, high = 2 * j + 1, 2 * j + 2
        packed[:, 2 * j * head_width : 2 * (j + 1) * head_width, :] = paired(
            dot(value_weight[degree_of(low)], features[low], 0, 0),
            dot(value_weight[degree_of(high)], features[high], 0, 0),
            head_width,
        )

    pl.semaphore_wait(barrier, len(greeted))

    for n in range(len(links)):
        scal_copy(n).start()
    for_points(lambda copy: copy.start())
    lead = 2
    for h in range(lead):
        for n in range(len(links)):
            value_copy(n, h).start()

    vals[group + mine, :, :sent] = packed[pl.ds(mine * heads, heads)]
    if relay:
        points[pl.ds(group * (1 - place), ranks)] = own_points[...]
    else:
        for s in range(slots):
            t = group * place - group + s

            @pl.when(jnp.logical_and(t >= 0, t < ranks))
            def _():
                points[s] = own_points[t]

    loads[3].wait()
    total_blocks = doms * ranks * per_tile
    lane = lax.broadcasted_iota(jnp.int32, (frames.shape[2], atoms), 1)
    frame_row = lax.broadcasted_iota(jnp.int32, (frames.shape[2], atoms), 0)
    slot_of = lax.broadcasted_iota(jnp.int32, (1, window * atoms), 1) // BLOCK

    def tables(q, carry):
        t = place * group + q
        points_t[q] = own_points[t].T
        wanted = jnp.zeros_like(lane) + frame_index[t * per_tile]
        for r in range(1, per_tile):
            wanted = jnp.where(lane < r * BLOCK, wanted, frame_index[t * per_tile + r])
        onehot = (frame_row == wanted).astype(jnp.float32)
        at = 0
        for l in range(degree_of(comp - 1) + 1):
            first, last = l * l, (l + 1) * (l + 1)
            kept = [
                lax.dot_general(
                    frames[j],
                    onehot,
                    (((1,), (0,)), ((), ())),
                    precision=lax.Precision.HIGHEST,
                    preferred_element_type=jnp.float32,
                )
                for j in range(first, last)
                if abs(j - first - l) <= 2
            ]
            for k in range(first, last):
                rows = None
                for matrix in kept:
                    term = matrix[k : k + 1, :] * matrix[first:last, :]
                    rows = term if rows is None else rows + term
                coef[q, at : at + last - first, :] = rows
                at += last - first
        for r in range(per_tile):
            block = t * per_tile + r
            hidden = jnp.full((1, window * atoms), FAR, jnp.float32)
            shift = r + group * per_tile - REACH
            for s in range(neighbours.shape[1]):
                offset = lax.rem(
                    neighbours[block, s]
                    - (dom * ranks * per_tile + block)
                    + REACH
                    + total_blocks,
                    total_blocks,
                )
                spot = jnp.where(counts[block] > s, offset + shift, -1)
                hidden = jnp.where(slot_of == spot, 0.0, hidden)
            mask[q, r : r + 1, :] = hidden
        return carry

    lax.fori_loop(0, group, tables, 0)

    for load in loads[4:]:
        load.wait()
    for k in range(comp):
        back[k] = (
            dot(output_weight[degree_of(k)], cotangent[k], 1, 0)
            .astype(jnp.bfloat16)
            .astype(jnp.float32)
        )
    strip = 4 * head_width

    def turn(i, carry):
        rows = pl.ds(pl.multiple_of(i * strip, strip), strip)

        def rotated(k):
            return rotated_rows(coef, mine, comp, lambda m: back[m, rows, :], k, True)

        into = pl.ds(i * 4, 4)
        for j in range((comp - 1) // 2):
            turned_out[into, 2 * j * head_width : 2 * (j + 1) * head_width, :] = paired(
                rotated(2 * j + 1), rotated(2 * j + 2), head_width
            )
        first = rotated(0)
        turned_out[into, sent : sent + 2 * head_width, :] = paired(
            first, jnp.zeros_like(first), head_width
        )
        return carry

    lax.fori_loop(0, channels // strip, turn, 0)

    for h in range(lead):
        for n in range(len(partners)):
            back_copy(n, h).start()
    for h in range(lead, heads):
        for n in range(len(links)):
            value_copy(n, h).start()
    for h in range(lead, heads):
        for n in range(len(partners)):
            back_copy(n, h).start()
    turned_in[mine] = turned_out[pl.ds(mine * heads, heads)]

    for n in range(len(links)):
        scal_arrival(n).wait_recv()
    if relay:
        for j in range(group):
            scal_forward(j).start()

    def prepare(slot, carry):
        tile = scal[slot]
        mixed = dot(value_weight[0], tile, 0, 0)
        chosen = mixed[:half]
        for n in range(1, group):
            chosen = jnp.where(mine == n, mixed[n * half : (n + 1) * half], chosen)
        vals[slot, :, sent : sent + 2 * head_width, :] = paired(
            chosen, jnp.zeros_like(chosen), head_width
        )
        keys = dot(k_weight[...], tile, 0, 0)
        keys_s[slot] = keys.reshape(heads, alpha, atoms).astype(jnp.bfloat16)
        return carry

    scale = 1.0 / math.sqrt(alpha)

    def ask(q, carry):
        turned = scal[group + q].astype(jnp.float32).T.astype(jnp.bfloat16)
        for h in range(heads):
            asked = dot(turned, q_weight[:, h * alpha : (h + 1) * alpha], 1, 0)
            queries_s[q, h] = (asked.astype(jnp.bfloat16).astype(jnp.float32) * scale).astype(
                jnp.bfloat16
            )
        return carry

    lax.fori_loop(0, group, ask, 0)
    if relay:
        start = group * (1 - place)
        lax.fori_loop(start, start + 2 * group, prepare, 0)
        for j in range(group):
            scal_forward(j).wait_recv()
        lax.fori_loop(near, near + group, prepare, 0)
    else:
        lax.fori_loop(0, slots, prepare, 0)
    for_points(lambda copy: copy.wait_recv())

    def windowed(q, get):
        return jnp.concatenate([get(q + w) for w in range(window)], axis=-1)

    def attend(q, carry):
        distance = None
        for c in range(3):
            row = windowed(q, lambda s: points[s, c : c + 1, :])
            apart = points_t[q, :, c : c + 1] - row
            distance = apart * apart if distance is None else distance + apart * apart
        hidden = jnp.concatenate(
            [
                jnp.broadcast_to(mask[q, r : r + 1, :], (BLOCK, window * atoms))
                for r in range(per_tile)
            ],
            axis=0,
        )
        distance_s[...] = jnp.maximum(distance, hidden)
        total_s[q] = jnp.zeros_like(distance)

        def head(c, carry):
            for h in (2 * c, 2 * c + 1):
                keys = windowed(q, lambda s: keys_s[s, h])
                strength = penalty[mine * heads + h]
                logits = dot(queries_s[q, h], keys, 1, 0) - strength * distance_s[...]
                peaks = jnp.max(logits, axis=1, keepdims=True)
                exponent = jnp.exp(logits - peaks)
                inverse = 1.0 / jnp.sum(exponent, axis=1, keepdims=True)
                attention = exponent * inverse
                attention_s[q, h] = attention
                rounded_s[q, h] = attention.astype(jnp.bfloat16)
            return carry

        return lax.fori_loop(0, heads // 2, head, carry)

    lax.fori_loop(0, group, attend, 0)

    crossing = len(links) - len(partners)

    def receive(h):
        for n in range(crossing):
            value_arrival(n, h).wait_recv()
        if relay:
            for j in range(group):
                value_forward(j, h).start()

    receive(0)

    last = heads // 2 - 1

    def finish(c):
        def rows_of(k):
            return (k - 1) * head_width if k else sent

        def rotated(q, k):
            def source(m):
                at = rows_of(m)
                return jnp.concatenate(
                    [aggregate_s[q, part, at : at + head_width, :] for part in range(2)], axis=0
                )

            return rotated_rows(coef, q, comp, source, k, False).astype(jnp.bfloat16)

        for n in range(len(partners)):
            q = partners[n][1]
            for k in range(comp):
                finished[n, c, k] = rotated(q, k)
            finished_copy(n, c).start()
        for k in range(comp):
            arrived[k, finished_rows(mine, c), :] = rotated(mine, k)

    def pair(c, carry):
        for part in range(2):
            h = 2 * c + part

            @pl.when(h + 1 < heads)
            def _():
                receive(h + 1)

            if relay:
                for j in range(group):
                    value_forward(j, h).wait_recv()
            for n in range(len(partners)):
                value_arrival(crossing + n, h).wait_recv()
                back_arrival(n, h).wait_recv()

            strength = 2.0 * penalty[mine * heads + h]

            def tile(q, carry):
                values = windowed(q, lambda s: vals[s, h])
                aggregate_s[q, part] = dot(values, rounded_s[q, h], 1, 1)
                turned = turned_in[q, h].astype(jnp.float32).T.astype(jnp.bfloat16)
                weight_grads = dot(turned, values, 1, 0)
                attention = attention_s[q, h]
                weighted = attention * weight_grads
                mean = jnp.sum(weighted, axis=1, keepdims=True)
                total_s[q] = total_s[q] + strength * (weighted - attention * mean)
                return carry

            for q in range(group):
                tile(q, 0)

        pl.when(c < last)(lambda: finish(c))
        return carry

    lax.fori_loop(0, heads // 2, pair, 0)

    forces[...] = jnp.zeros_like(forces)
    lane_square = lax.broadcasted_iota(jnp.int32, (atoms, atoms), 1)

    def pull(q, carry):
        total = total_s[q]
        own = jnp.zeros((atoms, atoms), jnp.float32)
        theirs = []
        for c in range(3):
            row = windowed(q, lambda s: points[s, c : c + 1, :])
            weighted = total * (points_t[q, :, c : c + 1] - row)
            own = jnp.where(lane_square == c, jnp.sum(weighted, axis=1, keepdims=True), own)
            theirs.append(jnp.sum(weighted, axis=0, keepdims=True))
        own = own.T
        for c in range(3):
            forces[q + group, c : c + 1, :] = forces[q + group, c : c + 1, :] + own[c : c + 1]
            for w in range(window):
                forces[q + w, c : c + 1, :] = (
                    forces[q + w, c : c + 1, :] - theirs[c][:, w * atoms : (w + 1) * atoms]
                )
        return carry

    for q in range(group):
        pull(q, 0)
    for n in range(len(others)):
        force_copy(n).start()
    finish(last)

    for n in range(len(links)):
        scal_copy(n).wait_send()
        for h in range(heads):
            value_copy(n, h).wait_send()
    if relay:
        for j in range(group):
            scal_forward(j).wait_send()
            for h in range(heads):
                value_forward(j, h).wait_send()
    for_points(lambda copy: copy.wait_send())
    for n in range(len(partners)):
        for h in range(heads):
            back_copy(n, h).wait_send()
    for n in range(len(partners)):
        for c in range(heads // 2):
            finished_arrival(n, c).wait_recv()
    for k in range(comp):
        mixed = dot(output_weight[degree_of(k)], arrived[k], 0, 0)
        updated[k] = (features[k].astype(jnp.float32) + mixed).astype(jnp.bfloat16)

    for n in range(len(others)):
        force_copy(n).wait_recv()
    summed = forces[group + mine]
    for n in range(len(others)):
        summed = summed + force_in[n]
    force[...] = summed[:3]

    for n in range(len(partners)):
        for c in range(heads // 2):
            finished_copy(n, c).wait_send()
    for n in range(len(others)):
        force_copy(n).wait_send()


def hand_over(pieces, updated_in, force_in, updated, force, sems, held, held_force):
    comp = updated.shape[0]
    fetches, stores = [], []
    for n in range(pieces):
        part = pl.ds(comp * n // pieces, comp * (n + 1) // pieces - comp * n // pieces)
        fetches.append(pltpu.make_async_copy(updated_in.at[part], held.at[part], sems.at[0, n]))
        stores.append(pltpu.make_async_copy(held.at[part], updated.at[part], sems.at[1, n]))
    fetches.append(pltpu.make_async_copy(force_in, held_force, sems.at[0, pieces]))
    stores.append(pltpu.make_async_copy(held_force, force, sems.at[1, pieces]))
    for fetch in fetches:
        fetch.start()
    for fetch, store in zip(fetches, stores):
        fetch.wait()
        store.start()
    for store in stores:
        store.wait()


def on_device(
    features,
    positions,
    penalty,
    qk_weight,
    value_weight,
    output_weight,
    frames,
    frame_index,
    neighbours,
    counts,
    cotangent,
):
    comp, channels, atoms = features.shape
    ranks = lax.axis_size("head")
    doms = lax.axis_size("dom")
    heads_all = penalty.shape[0]
    group = -(-REACH * BLOCK // atoms)
    heads = heads_all // group
    alpha = qk_weight.shape[1] // (2 * heads_all)
    head_width = channels // heads_all
    per_tile = atoms // BLOCK
    window = 2 * group + 1
    slots = 3 * group
    sent = (comp - 1) * head_width
    rows = sent + 2 * head_width
    others = 3 * group - 1
    links = 2 * group - 1 if ranks == 2 * group else others
    partners = group - 1
    table_rows = len(pair_table(comp))

    framed = frames.transpose(1, 2, 0)
    bf16, f32 = jnp.bfloat16, jnp.float32
    smem = pl.BlockSpec(memory_space=pltpu.SMEM)
    dma = pltpu.SemaphoreType.DMA
    updated, force = pl.pallas_call(
        functools.partial(fused_kernel, heads, alpha, doms, ranks, group),
        out_shape=(
            jax.ShapeDtypeStruct(features.shape, bf16),
            jax.ShapeDtypeStruct((positions.shape[0], atoms), f32),
        ),
        in_specs=[smem] * 4 + [pl.BlockSpec(memory_space=pltpu.MemorySpace.HBM)] * 7,
        out_specs=(vmem(), vmem()),
        scratch_shapes=[
            pltpu.VMEM((heads_all, sent, atoms), bf16),
            pltpu.VMEM((slots, heads, rows, atoms), bf16),
            pltpu.VMEM((slots, channels, atoms), bf16),
            pltpu.VMEM((comp, channels, atoms), f32),
            pltpu.VMEM((heads_all, rows, atoms), bf16),
            pltpu.VMEM((group, heads, rows, atoms), bf16),
            pltpu.VMEM((partners, heads // 2, comp, 2 * head_width, atoms), bf16),
            pltpu.VMEM((comp, channels, atoms), bf16),
            pltpu.VMEM((ranks, 8, atoms), f32),
            pltpu.VMEM((slots, 8, atoms), f32),
            pltpu.VMEM((group, atoms, 8), f32),
            pltpu.VMEM((group, table_rows, atoms), f32),
            pltpu.VMEM((group, per_tile, window * atoms), f32),
            pltpu.VMEM((atoms, window * atoms), f32),
            pltpu.VMEM((slots, heads, alpha, atoms), bf16),
            pltpu.VMEM((group, heads, atoms, alpha), bf16),
            pltpu.VMEM((group, 2, rows, atoms), f32),
            pltpu.VMEM((group, heads, atoms, window * atoms), f32),
            pltpu.VMEM((group, heads, atoms, window * atoms), bf16),
            pltpu.VMEM((group, atoms, window * atoms), f32),
            pltpu.VMEM((slots, 8, atoms), f32),
            pltpu.VMEM((others, 8, atoms), f32),
            dma((2, links)),
            dma((2, group)),
            dma((2, links, heads)),
            dma((2, group, heads)),
            dma((2, partners, heads)),
            dma((2, partners, heads // 2)),
            dma((2, others)),
            dma((2, 2)),
            pltpu.VMEM(features.shape, bf16),
            pltpu.VMEM(cotangent.shape, bf16),
            pltpu.VMEM(value_weight.shape, bf16),
            pltpu.VMEM(output_weight.shape, bf16),
            pltpu.VMEM((channels, heads * alpha), bf16),
            pltpu.VMEM((channels, heads * alpha), bf16),
            pltpu.VMEM(framed.shape, f32),
            pltpu.VMEM(positions.shape, f32),
            dma((8,)),
        ],
        compiler_params=pltpu.CompilerParams(
            vmem_limit_bytes=VMEM_LIMIT, collective_id=0, has_side_effects=True
        ),
        name="layer",
    )(
        penalty,
        frame_index,
        neighbours,
        counts,
        features,
        cotangent,
        value_weight,
        output_weight,
        qk_weight,
        framed,
        positions,
    )
    hbm = pl.BlockSpec(memory_space=pltpu.MemorySpace.HBM)
    return pl.pallas_call(
        functools.partial(hand_over, PIECES),
        out_shape=(
            jax.ShapeDtypeStruct(updated.shape, bf16),
            jax.ShapeDtypeStruct(force.shape, f32),
        ),
        in_specs=[hbm, hbm],
        out_specs=(hbm, hbm),
        scratch_shapes=[
            dma((2, PIECES + 1)),
            pltpu.VMEM(updated.shape, bf16),
            pltpu.VMEM(force.shape, f32),
        ],
        name="results",
    )(updated, force)


def solution(mesh):
    split = ("dom", "head")
    in_specs = (
        P(None, None, split),
        P(None, "dom"),
        P(),
        P(),
        P(),
        P(),
        P(),
        P("dom"),
        P("dom", None),
        P("dom"),
        P(None, None, split),
    )
    out_specs = (P(None, None, split), P(None, split))
    return jax.shard_map(
        on_device, mesh=mesh, in_specs=in_specs, out_specs=out_specs, check_vma=False
    )
```

```python
import functools
import math

import jax
import jax.numpy as jnp
from jax import lax
from jax.experimental import pallas as pl
from jax.experimental.pallas import tpu as pltpu
from jax.sharding import PartitionSpec as P

BLOCK = 64
REACH = 4
FAR = 1e30
VMEM_LIMIT = 63 * 1024 * 1024
PIECES = 5


def degree_of(k):
    return math.isqrt(k)


def pair_table(comp):
    pairs = []
    for k in range(comp):
        l = degree_of(k)
        for m in range(l * l, (l + 1) * (l + 1)):
            pairs.append((k, m))
    return pairs


def vmem():
    return pl.BlockSpec(memory_space=pltpu.VMEM)


def dot(a, b, ca, cb):
    return lax.dot_general(
        a, b, (((ca,), (cb,)), ((), ())), preferred_element_type=jnp.float32
    )


def rotated_rows(coef, tile, comp, source, k, turned):
    index_of = {pair: n for n, pair in enumerate(pair_table(comp))}
    l = degree_of(k)
    total = None
    for m in range(l * l, (l + 1) * (l + 1)):
        row = index_of[(m, k) if turned else (k, m)]
        term = coef[tile, row : row + 1, :] * source(m)
        total = term if total is None else total + term
    return total


def paired(low, high, head_width):
    rows, atoms = low.shape
    shape = (rows // head_width, head_width, atoms)
    return jnp.concatenate([low.reshape(shape), high.reshape(shape)], axis=1).astype(jnp.bfloat16)


def fused_kernel(
    heads,
    alpha,
    doms,
    ranks,
    group,
    penalty,
    frame_index,
    neighbours,
    counts,
    features_in,
    cotangent_in,
    value_weight_in,
    output_weight_in,
    qk_weight_in,
    frames_in,
    positions_in,
    updated,
    force,
    packed,
    vals,
    scal,
    back,
    turned_out,
    turned_in,
    finished,
    arrived,
    own_points,
    points,
    points_t,
    coef,
    mask,
    distance_s,
    keys_s,
    queries_s,
    aggregate_s,
    attention_s,
    rounded_s,
    total_s,
    forces,
    force_in,
    scal_sems,
    scal_forward_sems,
    value_sems,
    forward_sems,
    back_sems,
    finished_sems,
    force_sems,
    point_sems,
    features,
    cotangent,
    value_weight,
    output_weight,
    q_weight,
    k_weight,
    frames,
    positions,
    load_sems,
):
    comp, channels, atoms = features.shape
    head_width = channels // (group * heads)
    half = channels // group
    slots = 3 * group
    window = 2 * group + 1
    per_tile = atoms // BLOCK
    groups = ranks // group
    relay = groups == 2
    sent = (comp - 1) * head_width
    head_columns = heads * alpha
    me = lax.axis_index("head")
    dom = lax.axis_index("dom")
    mine = lax.rem(me, group)
    place = lax.div(me, group)
    up = lax.rem(dom + 1, doms)
    down = lax.rem(dom + doms - 1, doms)

    loads = [
        pltpu.make_async_copy(src, dst, load_sems.at[n])
        for n, (src, dst) in enumerate(
            [
                (features_in, features),
                (value_weight_in, value_weight),
                (positions_in, positions),
                (frames_in, frames),
                (cotangent_in, cotangent),
                (output_weight_in, output_weight),
                (
                    qk_weight_in.at[:, pl.ds(pl.multiple_of(mine * head_columns, 128), head_columns)],
                    q_weight,
                ),
                (
                    qk_weight_in.at[
                        :,
                        pl.ds(
                            pl.multiple_of((group + mine) * head_columns, 128), head_columns
                        ),
                    ],
                    k_weight,
                ),
            ]
        )
    ]
    for load in loads:
        load.start()

    def member(shift):
        return lax.rem(mine + shift, group)

    def group_at(shift):
        at = lax.rem(dom * groups + place + doms * groups + shift, doms * groups)
        return lax.div(at, groups), lax.rem(at, groups)

    others = []
    for shift, base in ((1, 2 * group), (-1, 0)):
        at_dom, at_place = group_at(shift)
        for j in range(group):
            n = member(j)
            others.append(
                (
                    (at_dom, at_place * group + n),
                    n,
                    base + n,
                    2 * group - base + mine,
                    2 * group - base + n,
                )
            )
    partners = []
    for j in range(1, group):
        n = member(j)
        partners.append(((dom, place * group + n), n, group + n, group + mine, group + n))
    others = others + partners

    far = 2 * group * (1 - place)
    near = 2 * group * place
    if relay:
        beside = lax.rem(dom + doms + 1 - 2 * place, doms)
        links = []
        for j in range(group):
            n = member(j)
            links.append(((dom, (1 - place) * group + n), n, far + n, near + mine, far + n))
        links = links + partners
    else:
        links = others

    def remote(src, dst, sems, at, device):
        return pltpu.make_async_remote_copy(
            src_ref=src,
            dst_ref=dst,
            send_sem=sems.at[(0,) + at],
            recv_sem=sems.at[(1,) + at],
            device_id=device,
            device_id_type=pl.DeviceIdType.MESH,
        )

    barrier = pltpu.get_barrier_semaphore()
    greeted = [other[0] for other in others] + [(up, me), (down, me)]
    for device in greeted:
        pl.semaphore_signal(
            barrier, inc=1, device_id=device, device_id_type=pl.DeviceIdType.MESH
        )

    def scal_copy(n):
        device, _, _, there, _ = links[n]
        return remote(scal.at[group + mine], scal.at[there], scal_sems, (n,), device)

    def scal_arrival(n):
        device, _, _, _, here = links[n]
        return remote(scal.at[group + mine], scal.at[here], scal_sems, (n,), device)

    def scal_forward(j):
        n = member(j)
        return remote(
            scal.at[far + n], scal.at[near + n], scal_forward_sems, (j,), (beside, me)
        )

    def value_copy(n, h):
        device, member_there, _, there, _ = links[n]
        return remote(
            packed.at[member_there * heads + h],
            vals.at[there, h, pl.ds(0, sent)],
            value_sems,
            (n, h),
            device,
        )

    def value_arrival(n, h):
        device, member_there, _, _, here = links[n]
        return remote(
            packed.at[member_there * heads + h],
            vals.at[here, h, pl.ds(0, sent)],
            value_sems,
            (n, h),
            device,
        )

    def value_forward(j, h):
        n = member(j)
        return remote(
            vals.at[far + n, h, pl.ds(0, sent)],
            vals.at[near + n, h, pl.ds(0, sent)],
            forward_sems,
            (j, h),
            (beside, me),
        )

    def back_copy(n, h):
        device, member_there, _, _, _ = partners[n]
        return remote(
            turned_out.at[member_there * heads + h], turned_in.at[mine, h], back_sems, (n, h), device
        )

    def back_arrival(n, h):
        device, member_there, _, _, _ = partners[n]
        return remote(
            turned_out.at[member_there * heads + h],
            turned_in.at[member_there, h],
            back_sems,
            (n, h),
            device,
        )

    def finished_rows(of, c):
        return pl.ds(pl.multiple_of(of * half + c * 2 * head_width, 16), 2 * head_width)

    def finished_copy(n, c):
        device, member_there, _, _, _ = partners[n]
        return remote(
            finished.at[n, c], arrived.at[:, finished_rows(mine, c)], finished_sems, (n, c), device
        )

    def finished_arrival(n, c):
        device, member_there, _, _, _ = partners[n]
        return remote(
            finished.at[n, c],
            arrived.at[:, finished_rows(member_there, c)],
            finished_sems,
            (n, c),
            device,
        )

    def force_copy(n):
        device, _, here, _, _ = others[n]
        return remote(forces.at[here], force_in.at[n], force_sems, (n,), device)

    if relay:
        point_copies = [
            (
                None,
                remote(
                    own_points.at[pl.ds((ranks - group) * (1 - place), group)],
                    points.at[pl.ds(near, group)],
                    point_sems,
                    (0,),
                    (beside, me),
                ),
            )
        ]
    else:
        point_copies = [
            (
                place == 0,
                remote(
                    own_points.at[pl.ds(ranks - group, group)],
                    points.at[pl.ds(0, group)],
                    point_sems,
                    (0,),
                    (up, me),
                ),
            ),
            (
                place == groups - 1,
                remote(
                    own_points.at[pl.ds(0, group)],
                    points.at[pl.ds(2 * group, group)],
                    point_sems,
                    (1,),
                    (down, me),
                ),
            ),
        ]

    def for_points(act):
        for holds, copy in point_copies:
            if holds is None:
                act(copy)
            else:
                pl.when(holds)(functools.partial(act, copy))

    for load in loads[:3]:
        load.wait()
    scal[group + mine] = features[0]
    own_points[...] = jnp.zeros_like(own_points)
    for t in range(ranks):
        own_points[t, : positions.shape[0]] = positions[:, t * atoms : (t + 1) * atoms]
    for j in range((comp - 1) // 2):
        low, high = 2 * j + 1, 2 * j + 2
        packed[:, 2 * j * head_width : 2 * (j + 1) * head_width, :] = paired(
            dot(value_weight[degree_of(low)], features[low], 0, 0),
            dot(value_weight[degree_of(high)], features[high], 0, 0),
            head_width,
        )

    pl.semaphore_wait(barrier, len(greeted))

    for n in range(len(links)):
        scal_copy(n).start()
    for_points(lambda copy: copy.start())
    lead = 2
    for h in range(lead):
        for n in range(len(links)):
            value_copy(n, h).start()

    vals[group + mine, :, :sent] = packed[pl.ds(mine * heads, heads)]
    if relay:
        points[pl.ds(group * (1 - place), ranks)] = own_points[...]
    else:
        for s in range(slots):
            t = group * place - group + s

            @pl.when(jnp.logical_and(t >= 0, t < ranks))
            def _():
                points[s] = own_points[t]

    loads[3].wait()
    total_blocks = doms * ranks * per_tile
    lane = lax.broadcasted_iota(jnp.int32, (frames.shape[2], atoms), 1)
    frame_row = lax.broadcasted_iota(jnp.int32, (frames.shape[2], atoms), 0)
    slot_of = lax.broadcasted_iota(jnp.int32, (1, window * atoms), 1) // BLOCK

    def tables(q, carry):
        t = place * group + q
        points_t[q] = own_points[t].T
        wanted = jnp.zeros_like(lane) + frame_index[t * per_tile]
        for r in range(1, per_tile):
            wanted = jnp.where(lane < r * BLOCK, wanted, frame_index[t * per_tile + r])
        onehot = (frame_row == wanted).astype(jnp.float32)
        at = 0
        for l in range(degree_of(comp - 1) + 1):
            first, last = l * l, (l + 1) * (l + 1)
            kept = [
                lax.dot_general(
                    frames[j],
                    onehot,
                    (((1,), (0,)), ((), ())),
                    precision=lax.Precision.HIGHEST,
                    preferred_element_type=jnp.float32,
                )
                for j in range(first, last)
                if abs(j - first - l) <= 2
            ]
            for k in range(first, last):
                rows = None
                for matrix in kept:
                    term = matrix[k : k + 1, :] * matrix[first:last, :]
                    rows = term if rows is None else rows + term
                coef[q, at : at + last - first, :] = rows
                at += last - first
        for r in range(per_tile):
            block = t * per_tile + r
            hidden = jnp.full((1, window * atoms), FAR, jnp.float32)
            shift = r + group * per_tile - REACH
            for s in range(neighbours.shape[1]):
                offset = lax.rem(
                    neighbours[block, s]
                    - (dom * ranks * per_tile + block)
                    + REACH
                    + total_blocks,
                    total_blocks,
                )
                spot = jnp.where(counts[block] > s, offset + shift, -1)
                hidden = jnp.where(slot_of == spot, 0.0, hidden)
            mask[q, r : r + 1, :] = hidden
        return carry

    lax.fori_loop(0, group, tables, 0)

    for load in loads[4:]:
        load.wait()
    for k in range(comp):
        back[k] = (
            dot(output_weight[degree_of(k)], cotangent[k], 1, 0)
            .astype(jnp.bfloat16)
            .astype(jnp.float32)
        )
    strip = 4 * head_width

    def turn(i, carry):
        rows = pl.ds(pl.multiple_of(i * strip, strip), strip)

        def rotated(k):
            return rotated_rows(coef, mine, comp, lambda m: back[m, rows, :], k, True)

        into = pl.ds(i * 4, 4)
        for j in range((comp - 1) // 2):
            turned_out[into, 2 * j * head_width : 2 * (j + 1) * head_width, :] = paired(
                rotated(2 * j + 1), rotated(2 * j + 2), head_width
            )
        first = rotated(0)
        turned_out[into, sent : sent + 2 * head_width, :] = paired(
            first, jnp.zeros_like(first), head_width
        )
        return carry

    lax.fori_loop(0, channels // strip, turn, 0)

    for h in range(lead):
        for n in range(len(partners)):
            back_copy(n, h).start()
    for h in range(lead, heads):
        for n in range(len(links)):
            value_copy(n, h).start()
    for h in range(lead, heads):
        for n in range(len(partners)):
            back_copy(n, h).start()
    turned_in[mine] = turned_out[pl.ds(mine * heads, heads)]

    for n in range(len(links)):
        scal_arrival(n).wait_recv()
    if relay:
        for j in range(group):
            scal_forward(j).start()

    def prepare(slot, carry):
        tile = scal[slot]
        mixed = dot(value_weight[0], tile, 0, 0)
        chosen = mixed[:half]
        for n in range(1, group):
            chosen = jnp.where(mine == n, mixed[n * half : (n + 1) * half], chosen)
        vals[slot, :, sent : sent + 2 * head_width, :] = paired(
            chosen, jnp.zeros_like(chosen), head_width
        )
        keys = dot(k_weight[...], tile, 0, 0)
        keys_s[slot] = keys.reshape(heads, alpha, atoms).astype(jnp.bfloat16)
        return carry

    scale = 1.0 / math.sqrt(alpha)

    def ask(q, carry):
        turned = scal[group + q].astype(jnp.float32).T.astype(jnp.bfloat16)
        for h in range(heads):
            asked = dot(turned, q_weight[:, h * alpha : (h + 1) * alpha], 1, 0)
            queries_s[q, h] = (asked.astype(jnp.bfloat16).astype(jnp.float32) * scale).astype(
                jnp.bfloat16
            )
        return carry

    lax.fori_loop(0, group, ask, 0)
    if relay:
        start = group * (1 - place)
        lax.fori_loop(start, start + 2 * group, prepare, 0)
        for j in range(group):
            scal_forward(j).wait_recv()
        lax.fori_loop(near, near + group, prepare, 0)
    else:
        lax.fori_loop(0, slots, prepare, 0)
    for_points(lambda copy: copy.wait_recv())

    def windowed(q, get):
        return jnp.concatenate([get(q + w) for w in range(window)], axis=-1)

    def attend(q, carry):
        distance = None
        for c in range(3):
            row = windowed(q, lambda s: points[s, c : c + 1, :])
            apart = points_t[q, :, c : c + 1] - row
            distance = apart * apart if distance is None else distance + apart * apart
        hidden = jnp.concatenate(
            [
                jnp.broadcast_to(mask[q, r : r + 1, :], (BLOCK, window * atoms))
                for r in range(per_tile)
            ],
            axis=0,
        )
        distance_s[...] = jnp.maximum(distance, hidden)
        total_s[q] = jnp.zeros_like(distance)

        def head(c, carry):
            for h in (2 * c, 2 * c + 1):
                keys = windowed(q, lambda s: keys_s[s, h])
                strength = penalty[mine * heads + h]
                logits = dot(queries_s[q, h], keys, 1, 0) - strength * distance_s[...]
                peaks = jnp.max(logits, axis=1, keepdims=True)
                exponent = jnp.exp(logits - peaks)
                inverse = 1.0 / jnp.sum(exponent, axis=1, keepdims=True)
                attention = exponent * inverse
                attention_s[q, h] = attention
                rounded_s[q, h] = attention.astype(jnp.bfloat16)
            return carry

        return lax.fori_loop(0, heads // 2, head, carry)

    lax.fori_loop(0, group, attend, 0)

    crossing = len(links) - len(partners)

    def receive(h):
        for n in range(crossing):
            value_arrival(n, h).wait_recv()
        if relay:
            for j in range(group):
                value_forward(j, h).start()

    receive(0)

    last = heads // 2 - 1

    def finish(c):
        def rows_of(k):
            return (k - 1) * head_width if k else sent

        def rotated(q, k):
            def source(m):
                at = rows_of(m)
                return jnp.concatenate(
                    [aggregate_s[q, part, at : at + head_width, :] for part in range(2)], axis=0
                )

            return rotated_rows(coef, q, comp, source, k, False).astype(jnp.bfloat16)

        for n in range(len(partners)):
            q = partners[n][1]
            for k in range(comp):
                finished[n, c, k] = rotated(q, k)
            finished_copy(n, c).start()
        for k in range(comp):
            arrived[k, finished_rows(mine, c), :] = rotated(mine, k)

    def pair(c, carry):
        for part in range(2):
            h = 2 * c + part

            if not isinstance(h, int) or h + 1 < heads:
                receive(h + 1)

            if relay:
                for j in range(group):
                    value_forward(j, h).wait_recv()
            for n in range(len(partners)):
                value_arrival(crossing + n, h).wait_recv()
                back_arrival(n, h).wait_recv()

            strength = 2.0 * penalty[mine * heads + h]

            def tile(q, carry):
                values = windowed(q, lambda s: vals[s, h])
                aggregate_s[q, part] = dot(values, rounded_s[q, h], 1, 1)
                turned = turned_in[q, h].astype(jnp.float32).T.astype(jnp.bfloat16)
                weight_grads = dot(turned, values, 1, 0)
                attention = attention_s[q, h]
                weighted = attention * weight_grads
                mean = jnp.sum(weighted, axis=1, keepdims=True)
                total_s[q] = total_s[q] + strength * (weighted - attention * mean)
                return carry

            for q in range(group):
                tile(q, 0)

        if not isinstance(c, int):
            finish(c)
        return carry

    lax.fori_loop(0, last, pair, 0)
    pair(last, 0)

    forces[...] = jnp.zeros_like(forces)
    lane_square = lax.broadcasted_iota(jnp.int32, (atoms, atoms), 1)

    def pull(q, carry):
        total = total_s[q]
        own = jnp.zeros((atoms, atoms), jnp.float32)
        theirs = []
        for c in range(3):
            row = windowed(q, lambda s: points[s, c : c + 1, :])
            weighted = total * (points_t[q, :, c : c + 1] - row)
            own = jnp.where(lane_square == c, jnp.sum(weighted, axis=1, keepdims=True), own)
            theirs.append(jnp.sum(weighted, axis=0, keepdims=True))
        own = own.T
        for c in range(3):
            forces[q + group, c : c + 1, :] = forces[q + group, c : c + 1, :] + own[c : c + 1]
            for w in range(window):
                forces[q + w, c : c + 1, :] = (
                    forces[q + w, c : c + 1, :] - theirs[c][:, w * atoms : (w + 1) * atoms]
                )
        return carry

    for q in range(group):
        pull(q, 0)
    for n in range(len(others)):
        force_copy(n).start()
    finish(last)

    for n in range(len(links)):
        scal_copy(n).wait_send()
        for h in range(heads):
            value_copy(n, h).wait_send()
    if relay:
        for j in range(group):
            scal_forward(j).wait_send()
            for h in range(heads):
                value_forward(j, h).wait_send()
    for_points(lambda copy: copy.wait_send())
    for n in range(len(partners)):
        for h in range(heads):
            back_copy(n, h).wait_send()
    for n in range(len(partners)):
        for c in range(heads // 2):
            finished_arrival(n, c).wait_recv()
    for k in range(comp):
        mixed = dot(output_weight[degree_of(k)], arrived[k], 0, 0)
        updated[k] = (features[k].astype(jnp.float32) + mixed).astype(jnp.bfloat16)

    for n in range(len(others)):
        force_copy(n).wait_recv()
    summed = forces[group + mine]
    for n in range(len(others)):
        summed = summed + force_in[n]
    force[...] = summed[:3]

    for n in range(len(partners)):
        for c in range(heads // 2):
            finished_copy(n, c).wait_send()
    for n in range(len(others)):
        force_copy(n).wait_send()


def hand_over(pieces, updated_in, force_in, updated, force, sems, held, held_force):
    comp = updated.shape[0]
    fetches, stores = [], []
    for n in range(pieces):
        part = pl.ds(comp * n // pieces, comp * (n + 1) // pieces - comp * n // pieces)
        fetches.append(pltpu.make_async_copy(updated_in.at[part], held.at[part], sems.at[0, n]))
        stores.append(pltpu.make_async_copy(held.at[part], updated.at[part], sems.at[1, n]))
    fetches.append(pltpu.make_async_copy(force_in, held_force, sems.at[0, pieces]))
    stores.append(pltpu.make_async_copy(held_force, force, sems.at[1, pieces]))
    for fetch in fetches:
        fetch.start()
    for fetch, store in zip(fetches, stores):
        fetch.wait()
        store.start()
    for store in stores:
        store.wait()


def on_device(
    features,
    positions,
    penalty,
    qk_weight,
    value_weight,
    output_weight,
    frames,
    frame_index,
    neighbours,
    counts,
    cotangent,
):
    comp, channels, atoms = features.shape
    ranks = lax.axis_size("head")
    doms = lax.axis_size("dom")
    heads_all = penalty.shape[0]
    group = -(-REACH * BLOCK // atoms)
    heads = heads_all // group
    alpha = qk_weight.shape[1] // (2 * heads_all)
    head_width = channels // heads_all
    per_tile = atoms // BLOCK
    window = 2 * group + 1
    slots = 3 * group
    sent = (comp - 1) * head_width
    rows = sent + 2 * head_width
    others = 3 * group - 1
    links = 2 * group - 1 if ranks == 2 * group else others
    partners = group - 1
    table_rows = len(pair_table(comp))

    framed = frames.transpose(1, 2, 0)
    bf16, f32 = jnp.bfloat16, jnp.float32
    smem = pl.BlockSpec(memory_space=pltpu.SMEM)
    dma = pltpu.SemaphoreType.DMA
    updated, force = pl.pallas_call(
        functools.partial(fused_kernel, heads, alpha, doms, ranks, group),
        out_shape=(
            jax.ShapeDtypeStruct(features.shape, bf16),
            jax.ShapeDtypeStruct((positions.shape[0], atoms), f32),
        ),
        in_specs=[smem] * 4 + [pl.BlockSpec(memory_space=pltpu.MemorySpace.HBM)] * 7,
        out_specs=(vmem(), vmem()),
        scratch_shapes=[
            pltpu.VMEM((heads_all, sent, atoms), bf16),
            pltpu.VMEM((slots, heads, rows, atoms), bf16),
            pltpu.VMEM((slots, channels, atoms), bf16),
            pltpu.VMEM((comp, channels, atoms), f32),
            pltpu.VMEM((heads_all, rows, atoms), bf16),
            pltpu.VMEM((group, heads, rows, atoms), bf16),
            pltpu.VMEM((partners, heads // 2, comp, 2 * head_width, atoms), bf16),
            pltpu.VMEM((comp, channels, atoms), bf16),
            pltpu.VMEM((ranks, 8, atoms), f32),
            pltpu.VMEM((slots, 8, atoms), f32),
            pltpu.VMEM((group, atoms, 8), f32),
            pltpu.VMEM((group, table_rows, atoms), f32),
            pltpu.VMEM((group, per_tile, window * atoms), f32),
            pltpu.VMEM((atoms, window * atoms), f32),
            pltpu.VMEM((slots, heads, alpha, atoms), bf16),
            pltpu.VMEM((group, heads, atoms, alpha), bf16),
            pltpu.VMEM((group, 2, rows, atoms), f32),
            pltpu.VMEM((group, heads, atoms, window * atoms), f32),
            pltpu.VMEM((group, heads, atoms, window * atoms), bf16),
            pltpu.VMEM((group, atoms, window * atoms), f32),
            pltpu.VMEM((slots, 8, atoms), f32),
            pltpu.VMEM((others, 8, atoms), f32),
            dma((2, links)),
            dma((2, group)),
            dma((2, links, heads)),
            dma((2, group, heads)),
            dma((2, partners, heads)),
            dma((2, partners, heads // 2)),
            dma((2, others)),
            dma((2, 2)),
            pltpu.VMEM(features.shape, bf16),
            pltpu.VMEM(cotangent.shape, bf16),
            pltpu.VMEM(value_weight.shape, bf16),
            pltpu.VMEM(output_weight.shape, bf16),
            pltpu.VMEM((channels, heads * alpha), bf16),
            pltpu.VMEM((channels, heads * alpha), bf16),
            pltpu.VMEM(framed.shape, f32),
            pltpu.VMEM(positions.shape, f32),
            dma((8,)),
        ],
        compiler_params=pltpu.CompilerParams(
            vmem_limit_bytes=VMEM_LIMIT, collective_id=0, has_side_effects=True
        ),
        name="layer",
    )(
        penalty,
        frame_index,
        neighbours,
        counts,
        features,
        cotangent,
        value_weight,
        output_weight,
        qk_weight,
        framed,
        positions,
    )
    hbm = pl.BlockSpec(memory_space=pltpu.MemorySpace.HBM)
    return pl.pallas_call(
        functools.partial(hand_over, PIECES),
        out_shape=(
            jax.ShapeDtypeStruct(updated.shape, bf16),
            jax.ShapeDtypeStruct(force.shape, f32),
        ),
        in_specs=[hbm, hbm],
        out_specs=(hbm, hbm),
        scratch_shapes=[
            dma((2, PIECES + 1)),
            pltpu.VMEM(updated.shape, bf16),
            pltpu.VMEM(force.shape, f32),
        ],
        name="results",
    )(updated, force)


def solution(mesh):
    split = ("dom", "head")
    in_specs = (
        P(None, None, split),
        P(None, "dom"),
        P(),
        P(),
        P(),
        P(),
        P(),
        P("dom"),
        P("dom", None),
        P("dom"),
        P(None, None, split),
    )
    out_specs = (P(None, None, split), P(None, split))
    return jax.shard_map(
        on_device, mesh=mesh, in_specs=in_specs, out_specs=out_specs, check_vma=False
    )
```

```python
import functools
import math

import jax
import jax.numpy as jnp
from jax import lax
from jax.experimental import pallas as pl
from jax.experimental.pallas import tpu as pltpu
from jax.sharding import PartitionSpec as P

BLOCK = 64
REACH = 4
FAR = 1e30
VMEM_LIMIT = 63 * 1024 * 1024
PIECES = 5


def degree_of(k):
    return math.isqrt(k)


def pair_table(comp):
    pairs = []
    for k in range(comp):
        l = degree_of(k)
        for m in range(l * l, (l + 1) * (l + 1)):
            pairs.append((k, m))
    return pairs


def vmem():
    return pl.BlockSpec(memory_space=pltpu.VMEM)


def dot(a, b, ca, cb):
    return lax.dot_general(
        a, b, (((ca,), (cb,)), ((), ())), preferred_element_type=jnp.float32
    )


def rotated_rows(coef, tile, comp, source, k, turned):
    index_of = {pair: n for n, pair in enumerate(pair_table(comp))}
    l = degree_of(k)
    total = None
    for m in range(l * l, (l + 1) * (l + 1)):
        row = index_of[(m, k) if turned else (k, m)]
        term = coef[tile, row : row + 1, :] * source(m)
        total = term if total is None else total + term
    return total


def paired(low, high, head_width):
    rows, atoms = low.shape
    shape = (rows // head_width, head_width, atoms)
    return jnp.concatenate([low.reshape(shape), high.reshape(shape)], axis=1).astype(jnp.bfloat16)


def fused_kernel(
    heads,
    alpha,
    doms,
    ranks,
    group,
    penalty,
    frame_index,
    neighbours,
    counts,
    features_in,
    cotangent_in,
    value_weight_in,
    output_weight_in,
    qk_weight_in,
    frames_in,
    positions_in,
    updated,
    force,
    packed,
    vals,
    scal,
    back,
    turned_out,
    turned_in,
    finished,
    arrived,
    own_points,
    points,
    points_t,
    coef,
    mask,
    distance_s,
    keys_s,
    queries_s,
    aggregate_s,
    attention_s,
    rounded_s,
    total_s,
    forces,
    force_in,
    scal_sems,
    scal_forward_sems,
    value_sems,
    forward_sems,
    back_sems,
    finished_sems,
    force_sems,
    point_sems,
    features,
    cotangent,
    value_weight,
    output_weight,
    q_weight,
    k_weight,
    frames,
    positions,
    load_sems,
):
    comp, channels, atoms = features.shape
    head_width = channels // (group * heads)
    half = channels // group
    slots = 3 * group
    window = 2 * group + 1
    per_tile = atoms // BLOCK
    groups = ranks // group
    relay = groups == 2
    sent = (comp - 1) * head_width
    head_columns = heads * alpha
    me = lax.axis_index("head")
    dom = lax.axis_index("dom")
    mine = lax.rem(me, group)
    place = lax.div(me, group)
    up = lax.rem(dom + 1, doms)
    down = lax.rem(dom + doms - 1, doms)

    loads = [
        pltpu.make_async_copy(src, dst, load_sems.at[n])
        for n, (src, dst) in enumerate(
            [
                (features_in, features),
                (value_weight_in, value_weight),
                (positions_in, positions),
                (frames_in, frames),
                (cotangent_in, cotangent),
                (output_weight_in, output_weight),
                (
                    qk_weight_in.at[:, pl.ds(pl.multiple_of(mine * head_columns, 128), head_columns)],
                    q_weight,
                ),
                (
                    qk_weight_in.at[
                        :,
                        pl.ds(
                            pl.multiple_of((group + mine) * head_columns, 128), head_columns
                        ),
                    ],
                    k_weight,
                ),
            ]
        )
    ]
    for load in loads:
        load.start()

    def member(shift):
        return lax.rem(mine + shift, group)

    def group_at(shift):
        at = lax.rem(dom * groups + place + doms * groups + shift, doms * groups)
        return lax.div(at, groups), lax.rem(at, groups)

    others = []
    for shift, base in ((1, 2 * group), (-1, 0)):
        at_dom, at_place = group_at(shift)
        for j in range(group):
            n = member(j)
            others.append(
                (
                    (at_dom, at_place * group + n),
                    n,
                    base + n,
                    2 * group - base + mine,
                    2 * group - base + n,
                )
            )
    partners = []
    for j in range(1, group):
        n = member(j)
        partners.append(((dom, place * group + n), n, group + n, group + mine, group + n))
    others = others + partners

    far = 2 * group * (1 - place)
    near = 2 * group * place
    if relay:
        beside = lax.rem(dom + doms + 1 - 2 * place, doms)
        links = []
        for j in range(group):
            n = member(j)
            links.append(((dom, (1 - place) * group + n), n, far + n, near + mine, far + n))
        links = links + partners
    else:
        links = others

    def remote(src, dst, sems, at, device):
        return pltpu.make_async_remote_copy(
            src_ref=src,
            dst_ref=dst,
            send_sem=sems.at[(0,) + at],
            recv_sem=sems.at[(1,) + at],
            device_id=device,
            device_id_type=pl.DeviceIdType.MESH,
        )

    barrier = pltpu.get_barrier_semaphore()
    greeted = [other[0] for other in others] + [(up, me), (down, me)]
    for device in greeted:
        pl.semaphore_signal(
            barrier, inc=1, device_id=device, device_id_type=pl.DeviceIdType.MESH
        )

    def scal_copy(n):
        device, _, _, there, _ = links[n]
        return remote(scal.at[group + mine], scal.at[there], scal_sems, (n,), device)

    def scal_arrival(n):
        device, _, _, _, here = links[n]
        return remote(scal.at[group + mine], scal.at[here], scal_sems, (n,), device)

    def scal_forward(j):
        n = member(j)
        return remote(
            scal.at[far + n], scal.at[near + n], scal_forward_sems, (j,), (beside, me)
        )

    def value_copy(n, h):
        device, member_there, _, there, _ = links[n]
        return remote(
            packed.at[member_there * heads + h],
            vals.at[there, h, pl.ds(0, sent)],
            value_sems,
            (n, h),
            device,
        )

    def value_arrival(n, h):
        device, member_there, _, _, here = links[n]
        return remote(
            packed.at[member_there * heads + h],
            vals.at[here, h, pl.ds(0, sent)],
            value_sems,
            (n, h),
            device,
        )

    def value_forward(j, h):
        n = member(j)
        return remote(
            vals.at[far + n, h, pl.ds(0, sent)],
            vals.at[near + n, h, pl.ds(0, sent)],
            forward_sems,
            (j, h),
            (beside, me),
        )

    def back_copy(n, h):
        device, member_there, _, _, _ = partners[n]
        return remote(
            turned_out.at[member_there * heads + h], turned_in.at[mine, h], back_sems, (n, h), device
        )

    def back_arrival(n, h):
        device, member_there, _, _, _ = partners[n]
        return remote(
            turned_out.at[member_there * heads + h],
            turned_in.at[member_there, h],
            back_sems,
            (n, h),
            device,
        )

    def finished_rows(of, c):
        return pl.ds(pl.multiple_of(of * half + c * 2 * head_width, 16), 2 * head_width)

    def finished_copy(n, c):
        device, member_there, _, _, _ = partners[n]
        return remote(
            finished.at[n, c], arrived.at[:, finished_rows(mine, c)], finished_sems, (n, c), device
        )

    def finished_arrival(n, c):
        device, member_there, _, _, _ = partners[n]
        return remote(
            finished.at[n, c],
            arrived.at[:, finished_rows(member_there, c)],
            finished_sems,
            (n, c),
            device,
        )

    def force_copy(n):
        device, _, here, _, _ = others[n]
        return remote(forces.at[here], force_in.at[n], force_sems, (n,), device)

    if relay:
        point_copies = [
            (
                None,
                remote(
                    own_points.at[pl.ds((ranks - group) * (1 - place), group)],
                    points.at[pl.ds(near, group)],
                    point_sems,
                    (0,),
                    (beside, me),
                ),
            )
        ]
    else:
        point_copies = [
            (
                place == 0,
                remote(
                    own_points.at[pl.ds(ranks - group, group)],
                    points.at[pl.ds(0, group)],
                    point_sems,
                    (0,),
                    (up, me),
                ),
            ),
            (
                place == groups - 1,
                remote(
                    own_points.at[pl.ds(0, group)],
                    points.at[pl.ds(2 * group, group)],
                    point_sems,
                    (1,),
                    (down, me),
                ),
            ),
        ]

    def for_points(act):
        for holds, copy in point_copies:
            if holds is None:
                act(copy)
            else:
                pl.when(holds)(functools.partial(act, copy))

    for load in loads[:3]:
        load.wait()
    scal[group + mine] = features[0]
    own_points[...] = jnp.zeros_like(own_points)
    for t in range(ranks):
        own_points[t, : positions.shape[0]] = positions[:, t * atoms : (t + 1) * atoms]
    for j in range((comp - 1) // 2):
        low, high = 2 * j + 1, 2 * j + 2
        packed[:, 2 * j * head_width : 2 * (j + 1) * head_width, :] = paired(
            dot(value_weight[degree_of(low)], features[low], 0, 0),
            dot(value_weight[degree_of(high)], features[high], 0, 0),
            head_width,
        )

    pl.semaphore_wait(barrier, len(greeted))

    for n in range(len(links)):
        scal_copy(n).start()
    for_points(lambda copy: copy.start())
    lead = 4
    for h in range(lead):
        for n in range(len(links)):
            value_copy(n, h).start()

    vals[group + mine, :, :sent] = packed[pl.ds(mine * heads, heads)]
    if relay:
        points[pl.ds(group * (1 - place), ranks)] = own_points[...]
    else:
        for s in range(slots):
            t = group * place - group + s

            @pl.when(jnp.logical_and(t >= 0, t < ranks))
            def _():
                points[s] = own_points[t]

    loads[3].wait()
    total_blocks = doms * ranks * per_tile
    lane = lax.broadcasted_iota(jnp.int32, (frames.shape[2], atoms), 1)
    frame_row = lax.broadcasted_iota(jnp.int32, (frames.shape[2], atoms), 0)
    slot_of = lax.broadcasted_iota(jnp.int32, (1, window * atoms), 1) // BLOCK

    def tables(q, carry):
        t = place * group + q
        points_t[q] = own_points[t].T
        wanted = jnp.zeros_like(lane) + frame_index[t * per_tile]
        for r in range(1, per_tile):
            wanted = jnp.where(lane < r * BLOCK, wanted, frame_index[t * per_tile + r])
        onehot = (frame_row == wanted).astype(jnp.float32)
        at = 0
        for l in range(degree_of(comp - 1) + 1):
            first, last = l * l, (l + 1) * (l + 1)
            kept = [
                lax.dot_general(
                    frames[j],
                    onehot,
                    (((1,), (0,)), ((), ())),
                    precision=lax.Precision.HIGHEST,
                    preferred_element_type=jnp.float32,
                )
                for j in range(first, last)
                if abs(j - first - l) <= 2
            ]
            for k in range(first, last):
                rows = None
                for matrix in kept:
                    term = matrix[k : k + 1, :] * matrix[first:last, :]
                    rows = term if rows is None else rows + term
                coef[q, at : at + last - first, :] = rows
                at += last - first
        for r in range(per_tile):
            block = t * per_tile + r
            hidden = jnp.full((1, window * atoms), FAR, jnp.float32)
            shift = r + group * per_tile - REACH
            for s in range(neighbours.shape[1]):
                offset = lax.rem(
                    neighbours[block, s]
                    - (dom * ranks * per_tile + block)
                    + REACH
                    + total_blocks,
                    total_blocks,
                )
                spot = jnp.where(counts[block] > s, offset + shift, -1)
                hidden = jnp.where(slot_of == spot, 0.0, hidden)
            mask[q, r : r + 1, :] = hidden
        return carry

    lax.fori_loop(0, group, tables, 0)

    for load in loads[4:]:
        load.wait()
    for k in range(comp):
        back[k] = (
            dot(output_weight[degree_of(k)], cotangent[k], 1, 0)
            .astype(jnp.bfloat16)
            .astype(jnp.float32)
        )
    strip = 4 * head_width

    def turn(i, carry):
        rows = pl.ds(pl.multiple_of(i * strip, strip), strip)

        def rotated(k):
            return rotated_rows(coef, mine, comp, lambda m: back[m, rows, :], k, True)

        into = pl.ds(i * 4, 4)
        for j in range((comp - 1) // 2):
            turned_out[into, 2 * j * head_width : 2 * (j + 1) * head_width, :] = paired(
                rotated(2 * j + 1), rotated(2 * j + 2), head_width
            )
        first = rotated(0)
        turned_out[into, sent : sent + 2 * head_width, :] = paired(
            first, jnp.zeros_like(first), head_width
        )
        return carry

    lax.fori_loop(0, channels // strip, turn, 0)

    for h in range(lead):
        for n in range(len(partners)):
            back_copy(n, h).start()
    for h in range(lead, heads):
        for n in range(len(links)):
            value_copy(n, h).start()
    for h in range(lead, heads):
        for n in range(len(partners)):
            back_copy(n, h).start()
    turned_in[mine] = turned_out[pl.ds(mine * heads, heads)]

    for n in range(len(links)):
        scal_arrival(n).wait_recv()
    if relay:
        for j in range(group):
            scal_forward(j).start()

    def prepare(slot, carry):
        tile = scal[slot]
        mixed = dot(value_weight[0], tile, 0, 0)
        chosen = mixed[:half]
        for n in range(1, group):
            chosen = jnp.where(mine == n, mixed[n * half : (n + 1) * half], chosen)
        vals[slot, :, sent : sent + 2 * head_width, :] = paired(
            chosen, jnp.zeros_like(chosen), head_width
        )
        keys = dot(k_weight[...], tile, 0, 0)
        keys_s[slot] = keys.reshape(heads, alpha, atoms).astype(jnp.bfloat16)
        return carry

    scale = 1.0 / math.sqrt(alpha)

    def ask(q, carry):
        turned = scal[group + q].astype(jnp.float32).T.astype(jnp.bfloat16)
        for h in range(heads):
            asked = dot(turned, q_weight[:, h * alpha : (h + 1) * alpha], 1, 0)
            queries_s[q, h] = (asked.astype(jnp.bfloat16).astype(jnp.float32) * scale).astype(
                jnp.bfloat16
            )
        return carry

    lax.fori_loop(0, group, ask, 0)
    if relay:
        start = group * (1 - place)
        lax.fori_loop(start, start + 2 * group, prepare, 0)
        for j in range(group):
            scal_forward(j).wait_recv()
        lax.fori_loop(near, near + group, prepare, 0)
    else:
        lax.fori_loop(0, slots, prepare, 0)
    for_points(lambda copy: copy.wait_recv())

    def windowed(q, get):
        return jnp.concatenate([get(q + w) for w in range(window)], axis=-1)

    def attend(q, carry):
        distance = None
        for c in range(3):
            row = windowed(q, lambda s: points[s, c : c + 1, :])
            apart = points_t[q, :, c : c + 1] - row
            distance = apart * apart if distance is None else distance + apart * apart
        hidden = jnp.concatenate(
            [
                jnp.broadcast_to(mask[q, r : r + 1, :], (BLOCK, window * atoms))
                for r in range(per_tile)
            ],
            axis=0,
        )
        distance_s[...] = jnp.maximum(distance, hidden)
        total_s[q] = jnp.zeros_like(distance)

        def head(c, carry):
            for h in (2 * c, 2 * c + 1):
                keys = windowed(q, lambda s: keys_s[s, h])
                strength = penalty[mine * heads + h]
                logits = dot(queries_s[q, h], keys, 1, 0) - strength * distance_s[...]
                peaks = jnp.max(logits, axis=1, keepdims=True)
                exponent = jnp.exp(logits - peaks)
                inverse = 1.0 / jnp.sum(exponent, axis=1, keepdims=True)
                attention = exponent * inverse
                attention_s[q, h] = attention
                rounded_s[q, h] = attention.astype(jnp.bfloat16)
            return carry

        return lax.fori_loop(0, heads // 2, head, carry)

    lax.fori_loop(0, group, attend, 0)

    crossing = len(links) - len(partners)

    def receive(h):
        for n in range(crossing):
            value_arrival(n, h).wait_recv()
        if relay:
            for j in range(group):
                value_forward(j, h).start()

    receive(0)

    last = heads // 2 - 1

    def finish(c):
        def rows_of(k):
            return (k - 1) * head_width if k else sent

        def rotated(q, k):
            def source(m):
                at = rows_of(m)
                return jnp.concatenate(
                    [aggregate_s[q, part, at : at + head_width, :] for part in range(2)], axis=0
                )

            return rotated_rows(coef, q, comp, source, k, False).astype(jnp.bfloat16)

        for n in range(len(partners)):
            q = partners[n][1]
            for k in range(comp):
                finished[n, c, k] = rotated(q, k)
            finished_copy(n, c).start()
        for k in range(comp):
            arrived[k, finished_rows(mine, c), :] = rotated(mine, k)

    def pair(c, carry):
        for part in range(2):
            h = 2 * c + part

            if not isinstance(h, int) or h + 1 < heads:
                receive(h + 1)

            if relay:
                for j in range(group):
                    value_forward(j, h).wait_recv()
            for n in range(len(partners)):
                value_arrival(crossing + n, h).wait_recv()
                back_arrival(n, h).wait_recv()

            strength = 2.0 * penalty[mine * heads + h]

            def tile(q, carry):
                values = windowed(q, lambda s: vals[s, h])
                aggregate_s[q, part] = dot(values, rounded_s[q, h], 1, 1)
                turned = turned_in[q, h].astype(jnp.float32).T.astype(jnp.bfloat16)
                weight_grads = dot(turned, values, 1, 0)
                attention = attention_s[q, h]
                weighted = attention * weight_grads
                mean = jnp.sum(weighted, axis=1, keepdims=True)
                total_s[q] = total_s[q] + strength * (weighted - attention * mean)
                return carry

            for q in range(group):
                tile(q, 0)

        if not isinstance(c, int):
            finish(c)
        return carry

    lax.fori_loop(0, last, pair, 0)
    pair(last, 0)

    forces[...] = jnp.zeros_like(forces)
    lane_square = lax.broadcasted_iota(jnp.int32, (atoms, atoms), 1)

    def pull(q, carry):
        total = total_s[q]
        own = jnp.zeros((atoms, atoms), jnp.float32)
        theirs = []
        for c in range(3):
            row = windowed(q, lambda s: points[s, c : c + 1, :])
            weighted = total * (points_t[q, :, c : c + 1] - row)
            own = jnp.where(lane_square == c, jnp.sum(weighted, axis=1, keepdims=True), own)
            theirs.append(jnp.sum(weighted, axis=0, keepdims=True))
        own = own.T
        for c in range(3):
            forces[q + group, c : c + 1, :] = forces[q + group, c : c + 1, :] + own[c : c + 1]
            for w in range(window):
                forces[q + w, c : c + 1, :] = (
                    forces[q + w, c : c + 1, :] - theirs[c][:, w * atoms : (w + 1) * atoms]
                )
        return carry

    for q in range(group):
        pull(q, 0)
    for n in range(len(others)):
        force_copy(n).start()
    finish(last)

    for n in range(len(links)):
        scal_copy(n).wait_send()
        for h in range(heads):
            value_copy(n, h).wait_send()
    if relay:
        for j in range(group):
            scal_forward(j).wait_send()
            for h in range(heads):
                value_forward(j, h).wait_send()
    for_points(lambda copy: copy.wait_send())
    for n in range(len(partners)):
        for h in range(heads):
            back_copy(n, h).wait_send()
    for n in range(len(partners)):
        for c in range(heads // 2):
            finished_arrival(n, c).wait_recv()
    for k in range(comp):
        mixed = dot(output_weight[degree_of(k)], arrived[k], 0, 0)
        updated[k] = (features[k].astype(jnp.float32) + mixed).astype(jnp.bfloat16)

    for n in range(len(others)):
        force_copy(n).wait_recv()
    summed = forces[group + mine]
    for n in range(len(others)):
        summed = summed + force_in[n]
    force[...] = summed[:3]

    for n in range(len(partners)):
        for c in range(heads // 2):
            finished_copy(n, c).wait_send()
    for n in range(len(others)):
        force_copy(n).wait_send()


def hand_over(pieces, updated_in, force_in, updated, force, sems, held, held_force):
    comp = updated.shape[0]
    fetches, stores = [], []
    for n in range(pieces):
        part = pl.ds(comp * n // pieces, comp * (n + 1) // pieces - comp * n // pieces)
        fetches.append(pltpu.make_async_copy(updated_in.at[part], held.at[part], sems.at[0, n]))
        stores.append(pltpu.make_async_copy(held.at[part], updated.at[part], sems.at[1, n]))
    fetches.append(pltpu.make_async_copy(force_in, held_force, sems.at[0, pieces]))
    stores.append(pltpu.make_async_copy(held_force, force, sems.at[1, pieces]))
    for fetch in fetches:
        fetch.start()
    for fetch, store in zip(fetches, stores):
        fetch.wait()
        store.start()
    for store in stores:
        store.wait()


def on_device(
    features,
    positions,
    penalty,
    qk_weight,
    value_weight,
    output_weight,
    frames,
    frame_index,
    neighbours,
    counts,
    cotangent,
):
    comp, channels, atoms = features.shape
    ranks = lax.axis_size("head")
    doms = lax.axis_size("dom")
    heads_all = penalty.shape[0]
    group = -(-REACH * BLOCK // atoms)
    heads = heads_all // group
    alpha = qk_weight.shape[1] // (2 * heads_all)
    head_width = channels // heads_all
    per_tile = atoms // BLOCK
    window = 2 * group + 1
    slots = 3 * group
    sent = (comp - 1) * head_width
    rows = sent + 2 * head_width
    others = 3 * group - 1
    links = 2 * group - 1 if ranks == 2 * group else others
    partners = group - 1
    table_rows = len(pair_table(comp))

    framed = frames.transpose(1, 2, 0)
    bf16, f32 = jnp.bfloat16, jnp.float32
    smem = pl.BlockSpec(memory_space=pltpu.SMEM)
    dma = pltpu.SemaphoreType.DMA
    updated, force = pl.pallas_call(
        functools.partial(fused_kernel, heads, alpha, doms, ranks, group),
        out_shape=(
            jax.ShapeDtypeStruct(features.shape, bf16),
            jax.ShapeDtypeStruct((positions.shape[0], atoms), f32),
        ),
        in_specs=[smem] * 4 + [pl.BlockSpec(memory_space=pltpu.MemorySpace.HBM)] * 7,
        out_specs=(vmem(), vmem()),
        scratch_shapes=[
            pltpu.VMEM((heads_all, sent, atoms), bf16),
            pltpu.VMEM((slots, heads, rows, atoms), bf16),
            pltpu.VMEM((slots, channels, atoms), bf16),
            pltpu.VMEM((comp, channels, atoms), f32),
            pltpu.VMEM((heads_all, rows, atoms), bf16),
            pltpu.VMEM((group, heads, rows, atoms), bf16),
            pltpu.VMEM((partners, heads // 2, comp, 2 * head_width, atoms), bf16),
            pltpu.VMEM((comp, channels, atoms), bf16),
            pltpu.VMEM((ranks, 8, atoms), f32),
            pltpu.VMEM((slots, 8, atoms), f32),
            pltpu.VMEM((group, atoms, 8), f32),
            pltpu.VMEM((group, table_rows, atoms), f32),
            pltpu.VMEM((group, per_tile, window * atoms), f32),
            pltpu.VMEM((atoms, window * atoms), f32),
            pltpu.VMEM((slots, heads, alpha, atoms), bf16),
            pltpu.VMEM((group, heads, atoms, alpha), bf16),
            pltpu.VMEM((group, 2, rows, atoms), f32),
            pltpu.VMEM((group, heads, atoms, window * atoms), f32),
            pltpu.VMEM((group, heads, atoms, window * atoms), bf16),
            pltpu.VMEM((group, atoms, window * atoms), f32),
            pltpu.VMEM((slots, 8, atoms), f32),
            pltpu.VMEM((others, 8, atoms), f32),
            dma((2, links)),
            dma((2, group)),
            dma((2, links, heads)),
            dma((2, group, heads)),
            dma((2, partners, heads)),
            dma((2, partners, heads // 2)),
            dma((2, others)),
            dma((2, 2)),
            pltpu.VMEM(features.shape, bf16),
            pltpu.VMEM(cotangent.shape, bf16),
            pltpu.VMEM(value_weight.shape, bf16),
            pltpu.VMEM(output_weight.shape, bf16),
            pltpu.VMEM((channels, heads * alpha), bf16),
            pltpu.VMEM((channels, heads * alpha), bf16),
            pltpu.VMEM(framed.shape, f32),
            pltpu.VMEM(positions.shape, f32),
            dma((8,)),
        ],
        compiler_params=pltpu.CompilerParams(
            vmem_limit_bytes=VMEM_LIMIT, collective_id=0, has_side_effects=True
        ),
        name="layer",
    )(
        penalty,
        frame_index,
        neighbours,
        counts,
        features,
        cotangent,
        value_weight,
        output_weight,
        qk_weight,
        framed,
        positions,
    )
    hbm = pl.BlockSpec(memory_space=pltpu.MemorySpace.HBM)
    return pl.pallas_call(
        functools.partial(hand_over, PIECES),
        out_shape=(
            jax.ShapeDtypeStruct(updated.shape, bf16),
            jax.ShapeDtypeStruct(force.shape, f32),
        ),
        in_specs=[hbm, hbm],
        out_specs=(hbm, hbm),
        scratch_shapes=[
            dma((2, PIECES + 1)),
            pltpu.VMEM(updated.shape, bf16),
            pltpu.VMEM(force.shape, f32),
        ],
        name="results",
    )(updated, force)


def solution(mesh):
    split = ("dom", "head")
    in_specs = (
        P(None, None, split),
        P(None, "dom"),
        P(),
        P(),
        P(),
        P(),
        P(),
        P("dom"),
        P("dom", None),
        P("dom"),
        P(None, None, split),
    )
    out_specs = (P(None, None, split), P(None, split))
    return jax.shard_map(
        on_device, mesh=mesh, in_specs=in_specs, out_specs=out_specs, check_vma=False
    )
```
